32 devices in a mesh: row: 8 (over y, x, core), col: 4 (over z).
Axes of the slice: x: 2, y: 2, z: 4, core: 2. Of those that a mesh axis runs over, the one named last changes fastest.
Arguments:
- features: bfloat16 [512, 256, 256], P('row', 'col'), may hold values from -6 to 6
- conv_expand: bfloat16 [256, 1024], replicated, may hold values from -0.375 to 0.375
- conv_kernel: bfloat16 [9, 1024], replicated, may hold values from -2 to 2
- conv_reduce: bfloat16 [1024, 256], replicated, may hold values from -0.1875 to 0.1875
- block_attend: bfloat16 [256, 768], replicated, as said below
- block_merge: bfloat16 [256, 256], replicated, may hold values from -0.375 to 0.375
- block_expand: bfloat16 [256, 1024], replicated, may hold values from -0.375 to 0.375
- block_reduce: bfloat16 [1024, 256], replicated, may hold values from -0.1875 to 0.1875
- grid_attend: bfloat16 [256, 768], replicated, as said below
- grid_merge: bfloat16 [256, 256], replicated, may hold values from -0.375 to 0.375
- grid_expand: bfloat16 [256, 1024], replicated, may hold values from -0.375 to 0.375
- grid_reduce: bfloat16 [1024, 256], replicated, may hold values from -0.1875 to 0.1875
- block_valid: int32 [64, 32], P('row', 'col'), may hold values from 0 to 1, as said below
- grid_valid: int32 [1, 64, 1, 32], P(None, 'row', None, 'col'), may hold values from 0 to 1, as said below
Outputs:
- output: bfloat16 [512, 256, 256], P('row', 'col')
The draws below stay inside these ranges and needn't reach their ends.
Inputs may be any that keep to these rules, and one draw needn't show every extreme that they name: `block_valid`: 1 marks a window whose tokens go through the section, 0 one whose tokens pass unchanged. `grid_valid`: 1 marks a window whose tokens go through the section, 0 one whose tokens pass unchanged. `block_attend`: columns are queries, keys and values. `grid_attend`: columns are queries, keys and values.
All inputs are finite; a program needn't handle non-finite values.
Results may differ from the reference program's by a relative error of at most 0.01.
Values may be sent and summed in bfloat16 or wider, within the bound.
No kernel may reach another device: no remote copies, remote signals or barrier semaphores. Data moves between devices by JAX's collectives and lax.ppermute only.
A program may use at most 192 MiB of HBM per device.

```python
import math
import jax
import jax.numpy as jnp
from jax import lax

C = 256
HEADS = 8
HEAD_DIM = 32
EXPAND = 1024
MLP = 1024
WIN = 8
GRID = 8
TILE_H = 64
IMG_H = 512
IMG_W = 256
BLK_ROWS = 64
BLK_COLS = 32
SPAN_H = 64
SPAN_W = 32
GQ_R = 1
GQ_C = 1


def paired_projection(key):
    pieces = jax.random.split(key, 3)
    spread = C ** (-0.5)
    query = jax.random.normal(pieces[0], (C, C), jnp.float32) * spread
    value = jax.random.normal(pieces[1], (C, C), jnp.float32) * spread
    noise = jax.random.normal(pieces[2], (C, C), jnp.float32) * spread
    key_part = noise
    return jnp.concatenate([query, key_part, value], axis=1).astype(jnp.bfloat16)


def draw_block_attend(key, part):
    return paired_projection(jax.random.fold_in(key, 11))


def draw_grid_attend(key, part):
    return paired_projection(jax.random.fold_in(key, 23))


def valid_region(key, row_total, col_total):
    pieces = jax.random.split(key, 3)
    live_rows = jax.random.randint(pieces[0], (), row_total // 4 + 1, row_total + 1)
    live_cols = jax.random.randint(pieces[1], (), col_total // 4 + 1, col_total + 1)
    holes = jax.random.randint(pieces[2], (row_total, col_total), 0, 8)
    inside = (jnp.arange(row_total)[:, None] < live_rows) & (jnp.arange(col_total)[None, :] < live_cols) & (holes > 0)
    return inside.astype(jnp.int32)


def draw_block_valid(key, part):
    return valid_region(jax.random.fold_in(key, 31), BLK_ROWS, BLK_COLS)


def draw_grid_valid(key, part):
    region = valid_region(jax.random.fold_in(key, 37), SPAN_H, SPAN_W)
    return region.reshape(GQ_R, SPAN_H // GQ_R, GQ_C, SPAN_W // GQ_C)


def steps_of(key, extent, cuts, smallest, largest):
    factor_of = 1.0
    for dim, shards_of in cuts:
        heights = jax.random.uniform(jax.random.fold_in(jax.random.fold_in(key, 6), dim), (shards_of,), jnp.float32, smallest / len(cuts), largest / len(cuts))
        factor_of = factor_of * jnp.repeat(jnp.exp(heights), extent[dim] // shards_of).reshape((-1,) + (1,) * (len(extent) - 1 - dim))
    return factor_of


def scatter_about(rng, shape, scale, bound, shards=(), kind=jnp.bfloat16):
    loudness = steps_of(rng, shape, shards, -0.22, 0.18) if shards else 1.0
    result = jax.random.normal(rng, shape, jnp.float32) * scale * loudness
    return jnp.minimum(jnp.maximum(result, -bound), bound).astype(kind)


def setup_inputs(seed: int = 0) -> dict:
    streams_of = jax.random.split(jax.random.key(seed), 15)
    features = scatter_about(streams_of[0], (IMG_H, IMG_W, C), 1.0, 6.0, ((0, 8), (1, 4)))
    conv_expand = scatter_about(streams_of[1], (C, EXPAND), C ** -0.5, 0.375)
    conv_kernel = scatter_about(streams_of[2], (9, EXPAND), 9 ** -0.5, 2.0)
    conv_reduce = scatter_about(streams_of[3], (EXPAND, C), EXPAND ** -0.5, 0.1875)
    block_attend = draw_block_attend(jax.random.fold_in(streams_of[14], 71), 0)
    block_merge = scatter_about(streams_of[5], (C, C), C ** -0.5, 0.375)
    block_expand = scatter_about(streams_of[6], (C, MLP), C ** -0.5, 0.375)
    block_reduce = scatter_about(streams_of[7], (MLP, C), MLP ** -0.5, 0.1875)
    grid_attend = draw_grid_attend(jax.random.fold_in(streams_of[14], 71), 0)
    grid_merge = scatter_about(streams_of[9], (C, C), C ** -0.5, 0.375)
    grid_expand = scatter_about(streams_of[10], (C, MLP), C ** -0.5, 0.375)
    grid_reduce = scatter_about(streams_of[11], (MLP, C), MLP ** -0.5, 0.1875)
    block_valid = draw_block_valid(jax.random.fold_in(streams_of[14], 71), 0)
    grid_valid = draw_grid_valid(jax.random.fold_in(streams_of[14], 71), 0)
    return dict(features=features, conv_expand=conv_expand, conv_kernel=conv_kernel, conv_reduce=conv_reduce, block_attend=block_attend, block_merge=block_merge, block_expand=block_expand, block_reduce=block_reduce, grid_attend=grid_attend, grid_merge=grid_merge, grid_expand=grid_expand, grid_reduce=grid_reduce, block_valid=block_valid, grid_valid=grid_valid)


EPSILON = 1e-05

def layer_norm(values):
    widened = values.astype(jnp.float32)
    centred = widened - lax.optimization_barrier(jnp.mean(widened, axis=-1, keepdims=True))
    variance = lax.optimization_barrier(jnp.mean(centred * centred, axis=-1, keepdims=True))
    return (centred * lax.rsqrt(variance + EPSILON)).astype(jnp.bfloat16)

def attend_windows(windows, attend, merge):
    window_count, tokens_per, channels = windows.shape
    normed = layer_norm(windows)
    packed = jnp.dot(normed.reshape(window_count * tokens_per, channels), attend, preferred_element_type=jnp.float32).astype(jnp.bfloat16)
    packed = packed.reshape(window_count, tokens_per, 3, HEADS, HEAD_DIM)
    scores = jnp.einsum('wqhd,wkhd->whqk', packed[:, :, 0].astype(jnp.float32), packed[:, :, 1].astype(jnp.float32)) * HEAD_DIM ** (-0.5)
    probs = jax.nn.softmax(scores, axis=-1).astype(jnp.bfloat16)
    mixed = jnp.einsum('whqk,wkhd->wqhd', probs.astype(jnp.float32), packed[:, :, 2].astype(jnp.float32)).astype(jnp.bfloat16)
    merged = jnp.dot(mixed.reshape(window_count * tokens_per, channels), merge, preferred_element_type=jnp.float32)
    return merged.reshape(window_count, tokens_per, channels)

def window_section(windows, flags, attend, merge, expand, reduce_weight):
    window_count, tokens_per, channels = windows.shape
    alive_mask = flags.astype(jnp.float32)[:, None, None]
    attended = (windows.astype(jnp.float32) + alive_mask * attend_windows(windows, attend, merge)).astype(jnp.bfloat16)
    normed = layer_norm(attended).reshape(window_count * tokens_per, channels)
    hidden = jax.nn.gelu(jnp.dot(normed, expand, preferred_element_type=jnp.float32), approximate=False).astype(jnp.bfloat16)
    reduced = jnp.dot(hidden, reduce_weight, preferred_element_type=jnp.float32).reshape(window_count, tokens_per, channels)
    return (attended.astype(jnp.float32) + alive_mask * reduced).astype(jnp.bfloat16)

def section_map(windows, flags, attend, merge, expand, reduce_weight):
    window_total = windows.shape[0]
    group = math.gcd(window_total, 64)
    shaped = windows.reshape(window_total // group, group, WIN * WIN, C)
    grouped_flags = flags.reshape(window_total // group, group)

    def one_group(inputs):
        return window_section(inputs[0], inputs[1], attend, merge, expand, reduce_weight)
    results = lax.map(one_group, (shaped, grouped_flags))
    return results.reshape(window_total, WIN * WIN, C)

def mbconv(features, conv_expand, conv_kernel, conv_reduce):
    height, breadth, channels = features.shape
    normed = layer_norm(features)
    padded = jnp.pad(normed, ((1, 1), (1, 1), (0, 0)))
    band_rows = TILE_H
    kernel_taps = conv_kernel.astype(jnp.float32)

    def one_band(band_index):
        first_row = band_index * band_rows
        slab_rows = lax.dynamic_slice_in_dim(padded, first_row, band_rows + 2, 0)
        expanded = jax.nn.gelu(jnp.dot(slab_rows.reshape(-1, channels), conv_expand, preferred_element_type=jnp.float32), approximate=False).astype(jnp.bfloat16)
        expanded = expanded.reshape(band_rows + 2, breadth + 2, EXPAND)
        summed = jnp.zeros((band_rows, breadth, EXPAND), jnp.float32)
        for position in range(9):
            shift_row = position // 3
            shift_col = position % 3
            summed = summed + expanded[shift_row:shift_row + band_rows, shift_col:shift_col + breadth].astype(jnp.float32) * kernel_taps[position]
        spatial = jax.nn.gelu(summed, approximate=False).astype(jnp.bfloat16)
        projected = jnp.dot(spatial.reshape(band_rows * breadth, EXPAND), conv_reduce, preferred_element_type=jnp.float32)
        residual_rows = lax.dynamic_slice_in_dim(features, first_row, band_rows, 0)
        return (residual_rows.astype(jnp.float32) + projected.reshape(band_rows, breadth, channels)).astype(jnp.bfloat16)
    bands = lax.map(one_band, jnp.arange(height // band_rows, dtype=jnp.int32))
    return bands.reshape(height, breadth, channels)

def reference(features, conv_expand, conv_kernel, conv_reduce, block_attend, block_merge, block_expand, block_reduce, grid_attend, grid_merge, grid_expand, grid_reduce, block_valid, grid_valid):
    height = IMG_H
    breadth = IMG_W
    after_conv = mbconv(features, conv_expand, conv_kernel, conv_reduce)
    blocks = after_conv.reshape(height // WIN, WIN, breadth // WIN, WIN, C).transpose(0, 2, 1, 3, 4).reshape(-1, WIN * WIN, C)
    sectioned = section_map(blocks, block_valid.reshape(-1), block_attend, block_merge, block_expand, block_reduce)
    after_block = sectioned.reshape(height // WIN, breadth // WIN, WIN, WIN, C).transpose(0, 2, 1, 3, 4).reshape(height, breadth, C)
    grids = after_block.reshape(GRID, SPAN_H, GRID, SPAN_W, C).transpose(1, 3, 0, 2, 4).reshape(-1, GRID * GRID, C)
    grid_flags = grid_valid.reshape(SPAN_H, SPAN_W).reshape(-1)
    finished = section_map(grids, grid_flags, grid_attend, grid_merge, grid_expand, grid_reduce)
    return finished.reshape(SPAN_H, SPAN_W, GRID, GRID, C).transpose(2, 0, 3, 1, 4).reshape(height, breadth, C)
```

```python
import functools

import jax
import jax.numpy as jnp
from jax import lax
from jax.experimental import pallas as pl
from jax.experimental.pallas import tpu as pltpu
from jax.sharding import PartitionSpec as P

HEADS = 8
WIN = 8
GRID = 8
EPSILON = 1e-05
LANES = 128
F32 = jnp.float32
BF16 = jnp.bfloat16


def dot(a, b):
    return jnp.dot(a, b, preferred_element_type=F32)


def dot_nt(a, b):
    return lax.dot_general(a, b, (((1,), (1,)), ((), ())), preferred_element_type=F32)


def gelu(x):
    return 0.5 * x * (1.0 + lax.erf(x * 0.7071067811865476))


def layer_norm(x):
    centred = x - jnp.mean(x, axis=-1, keepdims=True)
    variance = jnp.mean(centred * centred, axis=-1, keepdims=True)
    return (centred * lax.rsqrt(variance + EPSILON)).astype(BF16)


def section(x, flag_of, attend, merge, expand, reduce_weight):
    tokens, channels = x.shape
    per = WIN * WIN
    count = tokens // per
    head_width = channels // HEADS
    per_group = LANES // head_width
    groups = channels // LANES
    scale = head_width ** (-0.5) * 1.4426950408889634
    packed = dot(layer_norm(x), attend[...]).astype(BF16)
    lane = lax.broadcasted_iota(jnp.int32, (1, LANES), 1)
    masks = [jnp.where(lane // head_width == h, 1.0, 0.0).astype(BF16) for h in range(per_group)]
    low = lane < per
    row = lax.broadcasted_iota(jnp.int32, (per_group * per, LANES), 0)
    col = lax.broadcasted_iota(jnp.int32, (per_group * per, LANES), 1)
    ones = jnp.where(row // per == col // head_width, 1.0, 0.0).astype(BF16)
    mixed = []
    for g in range(groups):
        weights, tops = [], []
        for w in range(count):
            rows = slice(w * per, (w + 1) * per)
            q = packed[rows, g * LANES : (g + 1) * LANES]
            k = packed[rows, channels + g * LANES : channels + (g + 1) * LANES]
            v = packed[rows, 2 * channels + g * LANES : 2 * channels + (g + 1) * LANES]
            ks = jnp.concatenate([k * m for m in masks], axis=0)
            vs = jnp.concatenate([v * m for m in masks], axis=0)
            s = dot_nt(q, ks)
            parts = []
            for p in range(per_group * per // LANES):
                sp = s[:, p * LANES : (p + 1) * LANES]
                m0 = jnp.max(jnp.where(low, sp, -jnp.inf), axis=-1, keepdims=True)
                m1 = jnp.max(jnp.where(low, -jnp.inf, sp), axis=-1, keepdims=True)
                parts.append(jnp.exp2((sp - jnp.where(low, m0, m1)) * scale).astype(BF16))
            e = jnp.concatenate(parts, axis=1)
            weights.append(e)
            tops.append(dot(e, vs))
        total = dot(jnp.concatenate(weights, axis=0), ones)
        mixed.append((jnp.concatenate(tops, axis=0) / total).astype(BF16))
    merged = dot(jnp.concatenate(mixed, axis=1), merge[...])
    flags = [flag_of(w) for w in range(count)]

    def gated(base, update):
        return jnp.concatenate(
            [
                base[w * per : (w + 1) * per] + flags[w] * update[w * per : (w + 1) * per]
                for w in range(count)
            ],
            axis=0,
        )

    attended = gated(x, merged)
    normed = layer_norm(attended)
    hidden_width = expand.shape[1]
    step = min(256, hidden_width)
    reduced = None
    for start in range(0, hidden_width, step):
        hidden = gelu(dot(normed, expand[:, start : start + step])).astype(BF16)
        part = dot(hidden, reduce_weight[start : start + step, :])
        reduced = part if reduced is None else reduced + part
    return gated(attended, reduced)


def band_kernel(
    col_count,
    flags_ref,
    main_ref,
    above_ref,
    below_ref,
    top_ref,
    bottom_ref,
    sides_ref,
    conv_expand,
    conv_kernel,
    conv_reduce,
    attend,
    merge,
    expand,
    reduce_weight,
    out_ref,
):
    u = pl.program_id(0)
    last = pl.num_programs(0) - 1
    breadth, channels = main_ref.shape[1:]
    rows = WIN
    main = main_ref[...].astype(F32)
    above = jnp.where(u == 0, top_ref[...].astype(F32), above_ref[...].astype(F32))
    below = jnp.where(u == last, bottom_ref[...].astype(F32), below_ref[...].astype(F32))
    inner = (rows + 2) * breadth
    x = jnp.concatenate([above, main, below], axis=0).reshape(inner, channels)
    normed = layer_norm(jnp.concatenate([x, sides_ref[0].astype(F32)], axis=0))
    width = conv_expand.shape[1]
    step = min(256, width)
    column = lax.broadcasted_iota(jnp.int32, (1, breadth, 1), 1)
    first_col = column == 0
    last_col = column == breadth - 1
    taps = conv_kernel[...].astype(F32)
    projected = None
    for start in range(0, width, step):
        e = gelu(dot(normed, conv_expand[:, start : start + step]))
        body = e[:inner].reshape(rows + 2, breadth, step)
        side = e[inner:]
        sums, edges = [], []
        for j in range(3):
            k = [taps[3 * i + j : 3 * i + j + 1, start : start + step] for i in range(3)]
            sums.append(
                body[0:rows] * k[0] + body[1 : rows + 1] * k[1] + body[2 : rows + 2] * k[2]
            )
            if j != 1:
                part = side[:16] if j == 0 else side[16:]
                edge = part[0:rows] * k[0] + part[1 : rows + 1] * k[1] + part[2 : rows + 2] * k[2]
                edges.append(edge.reshape(rows, 1, step))
        left = jnp.where(first_col, edges[0], pltpu.roll(sums[0], 1, 1))
        right = jnp.where(last_col, edges[1], pltpu.roll(sums[2], breadth - 1, 1))
        spatial = gelu(sums[1] + left + right).reshape(rows * breadth, step).astype(BF16)
        part = dot(spatial, conv_reduce[start : start + step, :])
        projected = part if projected is None else projected + part
    after = main + projected.reshape(rows, breadth, channels)
    per_row = breadth // WIN
    x = jnp.concatenate(
        [
            after[:, v * WIN : (v + 1) * WIN].reshape(rows * WIN, channels)
            for v in range(per_row)
        ],
        axis=0,
    )

    out = section(
        x, lambda w: flags_ref[u, w].astype(F32), attend, merge, expand, reduce_weight
    )
    owners, _, owned, span, _ = out_ref.shape
    repeat = span // WIN
    for r in range(owners):
        for c in range(col_count):
            pieces = [
                out[(h * col_count + c) * WIN * WIN :][: WIN * WIN]
                .reshape(WIN, WIN, channels)[r * owned : (r + 1) * owned]
                for h in range(repeat)
            ]
            out_ref[r, c] = jnp.concatenate(pieces, axis=1).astype(BF16)


def grid_kernel(flags_ref, x_ref, attend, merge, expand, reduce_weight, out_ref):
    p, i = pl.program_id(0), pl.program_id(1)
    shape = x_ref.shape
    channels = shape[-1]
    tokens = WIN * GRID * GRID
    x = x_ref[...].reshape(tokens, channels)
    row = lax.broadcasted_iota(jnp.int32, (tokens, tokens), 0)
    col = lax.broadcasted_iota(jnp.int32, (tokens, tokens), 1)
    per = GRID * GRID
    order = jnp.where(col == (row % per) * WIN + row // per, 1.0, 0.0).astype(BF16)
    back = jnp.where(row == (col % per) * WIN + col // per, 1.0, 0.0).astype(BF16)
    out = section(
        dot(order, x),
        lambda w: flags_ref[p, i, w].astype(F32),
        attend,
        merge,
        expand,
        reduce_weight,
    )
    out_ref[...] = dot(back, out.astype(BF16)).astype(BF16).reshape(shape)


def whole(array):
    return pl.BlockSpec(array.shape, lambda *_: (0,) * array.ndim)


def shift(array, axis, up):
    size = lax.axis_size(axis)
    pairs = [(i, i + 1) for i in range(size - 1)]
    return lax.ppermute(array, axis, pairs if up else [(j, i) for i, j in pairs])


PARAMS = pltpu.CompilerParams(vmem_limit_bytes=56 << 20)


def conv_and_blocks(features, weights, flags, row_count, col_count):
    height, breadth, channels = features.shape
    bands = height // WIN
    top = shift(features[height - 1 :], "row", True)
    bottom = shift(features[:1], "row", False)
    edge_columns = [
        jnp.concatenate([top[:, c], features[:, c], bottom[:, c]], axis=0) for c in (0, breadth - 1)
    ]
    left = shift(edge_columns[1], "col", True)
    right = shift(edge_columns[0], "col", False)
    tall = WIN + 2
    gap = jnp.zeros((16 - tall, channels), BF16)
    sides = jnp.stack(
        [
            jnp.concatenate(
                [left[u * WIN : u * WIN + tall], gap, right[u * WIN : u * WIN + tall], gap]
            )
            for u in range(bands)
        ]
    )
    step_rows = height // row_count if height // row_count <= WIN else WIN
    owners = WIN // step_rows
    span = breadth // col_count
    in_specs = [
        pl.BlockSpec((WIN, breadth, channels), lambda u, f: (u, 0, 0)),
        pl.BlockSpec((1, breadth, channels), lambda u, f: (jnp.maximum(u * WIN - 1, 0), 0, 0)),
        pl.BlockSpec(
            (1, breadth, channels), lambda u, f: (jnp.minimum(u * WIN + WIN, height - 1), 0, 0)
        ),
        whole(top),
        whole(bottom),
        pl.BlockSpec((1, 32, channels), lambda u, f: (u, 0, 0)),
    ] + [whole(w) for w in weights]
    return pl.pallas_call(
        functools.partial(band_kernel, col_count),
        out_shape=jax.ShapeDtypeStruct((row_count, col_count, step_rows, span, channels), BF16),
        grid_spec=pltpu.PrefetchScalarGridSpec(
            num_scalar_prefetch=1,
            grid=(bands,),
            in_specs=in_specs,
            out_specs=pl.BlockSpec(
                (owners, col_count, step_rows, span, channels), lambda u, f: (u, 0, 0, 0, 0)
            ),
        ),
        compiler_params=PARAMS,
        name="conv_and_blocks",
    )(flags, features, features, features, top, bottom, sides, *weights)


def grid_section(arrived, weights, flags):
    shape = arrived.shape
    a, p, b, i, span, channels = shape
    spec = pl.BlockSpec((a, 1, b, 1, span, channels), lambda p, i, f: (0, p, 0, i, 0, 0))
    return pl.pallas_call(
        grid_kernel,
        out_shape=jax.ShapeDtypeStruct(shape, BF16),
        grid_spec=pltpu.PrefetchScalarGridSpec(
            num_scalar_prefetch=1,
            grid=(p, i),
            in_specs=[spec] + [whole(w) for w in weights],
            out_specs=spec,
        ),
        compiler_params=PARAMS,
        name="grid_section",
    )(flags, arrived, *weights)


def exchange(array):
    return lax.all_to_all(array, ("row", "col"), split_axis=0, concat_axis=0, tiled=True)


def on_device(
    features,
    conv_expand,
    conv_kernel,
    conv_reduce,
    block_attend,
    block_merge,
    block_expand,
    block_reduce,
    grid_attend,
    grid_merge,
    grid_expand,
    grid_reduce,
    block_valid,
    grid_valid,
):
    height, breadth, channels = features.shape
    rows, cols = lax.axis_size("row"), lax.axis_size("col")
    sending = conv_and_blocks(
        features,
        (
            conv_expand,
            conv_kernel,
            conv_reduce,
            block_attend,
            block_merge,
            block_expand,
            block_reduce,
        ),
        block_valid,
        rows,
        cols,
    )
    step_rows, span = sending.shape[2:4]
    parity = max(1, rows // GRID)
    arrived = exchange(sending.reshape(rows * cols, step_rows, span, channels))
    finished = grid_section(
        arrived.reshape(rows // parity, parity, cols, step_rows, span, channels),
        (grid_attend, grid_merge, grid_expand, grid_reduce),
        grid_valid.reshape(parity, step_rows, WIN),
    )
    returned = exchange(finished.reshape(rows * cols, step_rows, span, channels))
    spread = returned.reshape(rows, cols, step_rows, span // WIN, WIN, channels)
    return jnp.transpose(spread, (0, 2, 3, 1, 4, 5)).reshape(height, breadth, channels)


def solution(mesh):
    in_specs = (P("row", "col", None),) + (P(),) * 11 + (P("row", "col"), P(None, "row", None, "col"))
    return jax.shard_map(
        on_device,
        mesh=mesh,
        in_specs=in_specs,
        out_specs=P("row", "col", None),
        check_vma=False,
    )
```

```python
import functools

import jax
import jax.numpy as jnp
from jax import lax
from jax.experimental import pallas as pl
from jax.experimental.pallas import tpu as pltpu
from jax.sharding import PartitionSpec as P

HEADS = 8
WIN = 8
GRID = 8
PER = 64
EPSILON = 1e-05
LANES = 128
F32 = jnp.float32
BF16 = jnp.bfloat16
CHUNKS = 2
STEP_BANDS = 2


def dot(a, b):
    return jnp.dot(a, b, preferred_element_type=F32)


def dot_nt(a, b):
    return lax.dot_general(a, b, (((1,), (1,)), ((), ())), preferred_element_type=F32)


def gelu(x):
    return 0.5 * x * (1.0 + lax.erf(x * 0.7071067811865476))


def layer_norm(x):
    channels = x.shape[1]
    average = jnp.full((channels, LANES), 1.0 / channels, BF16)
    rounded = x.astype(BF16)
    mean = dot(rounded, average)
    wide = rounded.astype(F32)
    parts = [wide[:, s : s + LANES] - mean for s in range(0, channels, LANES)]
    squares = jnp.concatenate([(part * part).astype(BF16) for part in parts], axis=1)
    factor = lax.rsqrt(dot(squares, average) + EPSILON)
    return jnp.concatenate([(part * factor).astype(BF16) for part in parts], axis=1)


def attention(packed, count):
    channels = packed.shape[1] // 3
    head_width = channels // HEADS
    per_group = LANES // head_width
    groups = channels // LANES
    scale = head_width ** (-0.5) * 1.4426950408889634
    lane = lax.broadcasted_iota(jnp.int32, (1, LANES), 1)
    masks = [jnp.where(lane // head_width == h, 1.0, 0.0).astype(BF16) for h in range(per_group)]
    low = lane < PER
    row = lax.broadcasted_iota(jnp.int32, (per_group * PER, LANES), 0)
    col = lax.broadcasted_iota(jnp.int32, (per_group * PER, LANES), 1)
    ones = jnp.where(row // PER == col // head_width, 1.0, 0.0).astype(BF16)

    def piece(kind, w, g):
        start = kind * channels + g * LANES
        return packed[w * PER : (w + 1) * PER, start : start + LANES]

    def by_head(x):
        return jnp.concatenate([x * m for m in masks], axis=0)

    items = [(w, g) for g in range(groups) for w in range(count)]
    scores = [dot_nt(piece(0, w, g), by_head(piece(1, w, g))) for w, g in items]
    weights = []
    for s in scores:
        parts = []
        for p in range(per_group * PER // LANES):
            sp = s[:, p * LANES : (p + 1) * LANES]
            m0 = jnp.max(jnp.where(low, sp, -jnp.inf), axis=-1, keepdims=True)
            m1 = jnp.max(jnp.where(low, -jnp.inf, sp), axis=-1, keepdims=True)
            parts.append(jnp.exp2((sp - jnp.where(low, m0, m1)) * scale).astype(BF16))
        weights.append(jnp.concatenate(parts, axis=1))
    total = dot(jnp.concatenate(weights, axis=0), ones)
    tops = [dot(e, by_head(piece(2, w, g))) for (w, g), e in zip(items, weights)]
    mixed = (jnp.concatenate(tops, axis=0) / total).astype(BF16)
    size = count * PER
    return jnp.concatenate([mixed[g * size : (g + 1) * size] for g in range(groups)], axis=1)


def section(x, flags, attend, merge, expand, reduce_weight):
    count = x.shape[0] // PER

    def gated(base, update):
        return jnp.concatenate(
            [
                base[w * PER : (w + 1) * PER] + flags[w] * update[w * PER : (w + 1) * PER]
                for w in range(count)
            ],
            axis=0,
        )

    packed = dot(layer_norm(x), attend[...]).astype(BF16)
    attended = gated(x, dot(attention(packed, count), merge[...]))
    normed = layer_norm(attended)
    hidden_width = expand.shape[1]
    step = min(256, hidden_width)
    reduced = None
    for start in range(0, hidden_width, step):
        hidden = gelu(dot(normed, expand[:, start : start + step])).astype(BF16)
        part = dot(hidden, reduce_weight[start : start + step, :])
        reduced = part if reduced is None else reduced + part
    return gated(attended, reduced)


def mbconv(main, above, below, sides, conv_expand, conv_kernel, conv_reduce):
    rows, breadth, channels = main.shape
    inner = (rows + 2) * breadth
    side_rows = sides.shape[0] // 2
    x = jnp.concatenate([above, main, below], axis=0).reshape(inner, channels)
    normed = layer_norm(jnp.concatenate([x, sides], axis=0))
    width = conv_expand.shape[1]
    step = min(256, width)
    column = lax.broadcasted_iota(jnp.int32, (1, breadth, 1), 1)
    first_col = column == 0
    last_col = column == breadth - 1
    taps = conv_kernel[...].astype(F32)
    projected = None
    for start in range(0, width, step):
        e = gelu(dot(normed, conv_expand[:, start : start + step]))
        body = e[:inner].reshape(rows + 2, breadth, step)
        side = e[inner:]
        sums, edges = [], []
        for j in range(3):
            k = [taps[3 * i + j : 3 * i + j + 1, start : start + step] for i in range(3)]
            sums.append(
                body[0:rows] * k[0] + body[1 : rows + 1] * k[1] + body[2 : rows + 2] * k[2]
            )
            if j != 1:
                part = side[:side_rows] if j == 0 else side[side_rows:]
                edge = part[0:rows] * k[0] + part[1 : rows + 1] * k[1] + part[2 : rows + 2] * k[2]
                edges.append(edge.reshape(rows, 1, step))
        left = jnp.where(first_col, edges[0], pltpu.roll(sums[0], 1, 1))
        right = jnp.where(last_col, edges[1], pltpu.roll(sums[2], breadth - 1, 1))
        spatial = gelu(sums[1] + left + right).reshape(rows * breadth, step).astype(BF16)
        part = dot(spatial, conv_reduce[start : start + step, :])
        projected = part if projected is None else projected + part
    return main + projected.reshape(rows, breadth, channels)


def band_kernel(
    first_band,
    direct,
    flags_ref,
    main_ref,
    above_ref,
    below_ref,
    top_ref,
    bottom_ref,
    sides_ref,
    conv_expand,
    conv_kernel,
    conv_reduce,
    attend,
    merge,
    expand,
    reduce_weight,
    out_ref,
):
    rows, breadth, channels = main_ref.shape
    bands, per_row = rows // WIN, breadth // WIN
    step = pl.program_id(0)
    first_band = first_band + step * bands
    last_band = flags_ref.shape[0] - bands
    above = jnp.where(first_band == 0, top_ref[...].astype(F32), above_ref[...].astype(F32))
    below = jnp.where(
        first_band == last_band, bottom_ref[...].astype(F32), below_ref[...].astype(F32)
    )
    after = mbconv(
        main_ref[...].astype(F32),
        above,
        below,
        sides_ref[0].astype(F32),
        conv_expand,
        conv_kernel,
        conv_reduce,
    )
    windows = [(t, v) for t in range(bands) for v in range(per_row)]
    x = jnp.concatenate(
        [
            after[t * WIN : (t + 1) * WIN, v * WIN : (v + 1) * WIN].reshape(PER, channels)
            for t, v in windows
        ],
        axis=0,
    )
    flags = [flags_ref[first_band + t, v].astype(F32) for t, v in windows]
    out = section(x, flags, attend, merge, expand, reduce_weight)
    square = {
        tv: out[n * PER : (n + 1) * PER].reshape(WIN, WIN, channels)
        for n, tv in enumerate(windows)
    }
    if direct:
        cols = out_ref.shape[1]
        for t in range(bands):
            for c in range(cols):
                pieces = [square[t, v] for v in range(c, per_row, cols)]
                out_ref[:, c, t] = jnp.concatenate(pieces, axis=1).astype(BF16)
    else:
        for t in range(bands):
            pieces = [square[t, v] for v in range(per_row)]
            out_ref[t * WIN : (t + 1) * WIN] = jnp.concatenate(pieces, axis=1).astype(BF16)


def grid_kernel(first_band, direct, flags_ref, x_ref, attend, merge, expand, reduce_weight, out_ref):
    channels = x_ref.shape[-1]
    tokens = WIN * PER
    first_band = first_band + pl.program_id(0) * STEP_BANDS
    if direct:
        bands = x_ref.shape[1]
        row = lax.broadcasted_iota(jnp.int32, (tokens, tokens), 0)
        col = lax.broadcasted_iota(jnp.int32, (tokens, tokens), 1)
        order = jnp.where(col == (row % PER) * WIN + row // PER, 1.0, 0.0).astype(BF16)
        back = jnp.where(row == (col % PER) * WIN + col // PER, 1.0, 0.0).astype(BF16)
        x = [dot(order, x_ref[:, t].reshape(tokens, channels)) for t in range(bands)]
    else:
        bands = x_ref.shape[0]
        x = [x_ref[t].astype(F32) for t in range(bands)]
    flags = [flags_ref[first_band + t, w].astype(F32) for t in range(bands) for w in range(WIN)]
    out = section(jnp.concatenate(x, axis=0), flags, attend, merge, expand, reduce_weight)
    for t in range(bands):
        part = out[t * tokens : (t + 1) * tokens].astype(BF16)
        if direct:
            out_ref[:, t] = dot(back, part).astype(BF16).reshape(out_ref[:, t].shape)
        else:
            out_ref[t] = part


def whole(array):
    return pl.BlockSpec(array.shape, lambda *_: (0,) * array.ndim)


def shift(array, axis, up):
    size = lax.axis_size(axis)
    pairs = [(i, i + 1) for i in range(size - 1)]
    return lax.ppermute(array, axis, pairs if up else [(j, i) for i, j in pairs])


PARAMS = pltpu.CompilerParams(vmem_limit_bytes=60 << 20)


def along(shape, axis, size):
    block = shape[:axis] + (size,) + shape[axis + 1 :]
    return pl.BlockSpec(
        block, lambda i, f: (0,) * axis + (i,) + (0,) * (len(shape) - axis - 1)
    )


def call(kernel, steps, flags, specs, arrays, shape, out_spec, name):
    return pl.pallas_call(
        kernel,
        out_shape=jax.ShapeDtypeStruct(shape, BF16),
        grid_spec=pltpu.PrefetchScalarGridSpec(
            num_scalar_prefetch=1, grid=(steps,), in_specs=specs, out_specs=out_spec
        ),
        compiler_params=PARAMS,
        name=name,
    )(flags, *arrays)


def feature_halo(features, beside):
    height, breadth, _ = features.shape
    top = shift(features[height - 1 :], "row", True)
    bottom = shift(features[:1], "row", False)
    edge_columns = [
        jnp.concatenate([top[:, c], features[:, c], bottom[:, c]], axis=0) for c in (0, breadth - 1)
    ]
    edge_columns, beside = lax.optimization_barrier((edge_columns, beside))
    left = shift(edge_columns[1], "col", True)
    right = shift(edge_columns[0], "col", False)
    return top, bottom, left, right, beside


def exchange(array):
    return lax.all_to_all(array, ("row", "col"), split_axis=0, concat_axis=0, tiled=True)


def on_device(
    features,
    conv_expand,
    conv_kernel,
    conv_reduce,
    block_attend,
    block_merge,
    block_expand,
    block_reduce,
    grid_attend,
    grid_merge,
    grid_expand,
    grid_reduce,
    block_valid,
    grid_valid,
):
    height, breadth, channels = features.shape
    rows, cols = lax.axis_size("row"), lax.axis_size("col")
    devices = rows * cols
    parity = rows // GRID
    repeat = breadth // (WIN * cols)
    part = WIN // parity
    direct = parity == 1
    per_chunk = height // WIN // CHUNKS
    tall = per_chunk * WIN

    me = lax.axis_index("row")
    gathered = lax.all_gather(grid_valid[:, :, 0, :], "row", axis=1, tiled=True)
    by_band = gathered.reshape(parity, height // WIN, WIN, WIN)
    mine = lax.dynamic_index_in_dim(by_band, me // parity, 2, keepdims=False)
    mine = lax.dynamic_slice_in_dim(mine, (me % parity) * part, part, 2)
    grid_flags = jnp.transpose(mine, (1, 0, 2)).reshape(height // WIN, WIN)

    top, bottom, left, right, grid_flags = feature_halo(features, grid_flags)
    conv_weights = (conv_expand, conv_kernel, conv_reduce)
    block_weights = (block_attend, block_merge, block_expand, block_reduce)
    grid_weights = (grid_attend, grid_merge, grid_expand, grid_reduce)
    steps = per_chunk // STEP_BANDS
    step_rows = STEP_BANDS * WIN
    padded = -(-(step_rows + 2) // 8) * 8
    gap = jnp.zeros((padded - step_rows - 2, channels), BF16)
    row_block = (1, breadth, channels)

    outputs = []
    for k in range(CHUNKS):
        low = k * tall
        sides = jnp.stack(
            [
                jnp.concatenate([left[r : r + step_rows + 2], gap, right[r : r + step_rows + 2], gap])
                for r in range(low, low + tall, step_rows)
            ]
        )
        arrays = [features, features, features, top, bottom, sides, *conv_weights, *block_weights]

        def row_at(offset, k=k):
            def index(i, f):
                row = (k * steps + i) * step_rows + offset
                return jnp.clip(row, 0, height - 1), 0, 0

            return pl.BlockSpec(row_block, index)

        specs = [
            pl.BlockSpec((step_rows, breadth, channels), lambda i, f, k=k: (k * steps + i, 0, 0)),
            row_at(-1),
            row_at(step_rows),
            whole(top),
            whole(bottom),
            along(sides.shape, 0, 1),
        ] + [whole(a) for a in arrays[6:]]
        if direct:
            shape = (rows, cols, per_chunk, repeat * WIN, channels)
            out_spec = along(shape, 2, STEP_BANDS)
        else:
            shape = (tall, breadth, channels)
            out_spec = along(shape, 0, step_rows)
        sending = call(
            functools.partial(band_kernel, k * per_chunk, direct),
            steps,
            block_valid,
            specs,
            arrays,
            shape,
            out_spec,
            "conv_and_blocks",
        )
        if not direct:
            split = sending.reshape(per_chunk, WIN, repeat, cols, parity, part, channels)
            sending = jnp.transpose(split, (1, 4, 3, 0, 2, 5, 6))
        arrived = exchange(sending.reshape(devices, per_chunk, repeat * part, channels))
        if not direct:
            split = arrived.reshape(GRID, parity, cols, per_chunk, repeat, part, channels)
            arrived = jnp.transpose(split, (3, 1, 5, 0, 2, 4, 6))
            arrived = arrived.reshape(per_chunk, WIN * PER, channels)
        arrays = [arrived, *grid_weights]
        spec = along(arrived.shape, 1 if direct else 0, STEP_BANDS)
        finished = call(
            functools.partial(grid_kernel, k * per_chunk, direct),
            steps,
            grid_flags,
            [spec] + [whole(a) for a in grid_weights],
            arrays,
            arrived.shape,
            spec,
            "grid_section",
        )
        if not direct:
            split = finished.reshape(per_chunk, parity, part, GRID, cols, repeat, channels)
            finished = jnp.transpose(split, (3, 1, 4, 0, 5, 2, 6))
        returned = exchange(finished.reshape(devices, per_chunk, repeat * part, channels))
        split = returned.reshape(WIN, parity, cols, per_chunk, repeat, part, channels)
        spread = jnp.transpose(split, (3, 0, 4, 2, 1, 5, 6))
        outputs.append(spread.reshape(tall, breadth, channels))
    return jnp.concatenate(outputs, axis=0)


def solution(mesh):
    in_specs = (P("row", "col", None),) + (P(),) * 11
    in_specs += (P("row", "col"), P(None, "row", None, "col"))
    return jax.shard_map(
        on_device,
        mesh=mesh,
        in_specs=in_specs,
        out_specs=P("row", "col", None),
        check_vma=False,
    )
```

```python
import functools

import jax
import jax.numpy as jnp
from jax import lax
from jax.experimental import pallas as pl
from jax.experimental.pallas import tpu as pltpu
from jax.sharding import PartitionSpec as P

HEADS = 8
WIN = 8
GRID = 8
PER = 64
EPSILON = 1e-05
LANES = 128
F32 = jnp.float32
BF16 = jnp.bfloat16
CHUNKS = 2
STEP_BANDS = 2
PLACES = 4


def dot(a, b):
    return jnp.dot(a, b, preferred_element_type=F32)


def dot_nt(a, b):
    return lax.dot_general(a, b, (((1,), (1,)), ((), ())), preferred_element_type=F32)


HALF_ROOT = 0.7071067811865476


def gelu_scaled(y):
    return y + y * lax.erf(y)


def layer_norm(x, scale=1.0):
    channels = x.shape[1]
    average = jnp.full((channels, LANES), 1.0 / channels, BF16)
    rounded = x.astype(BF16)
    mean = dot(rounded, average)
    wide = rounded.astype(F32)
    parts = [wide[:, s : s + LANES] - mean for s in range(0, channels, LANES)]
    squares = jnp.concatenate([(part * part).astype(BF16) for part in parts], axis=1)
    factor = lax.rsqrt(dot(squares, average) + EPSILON) * scale
    return jnp.concatenate([(part * factor).astype(BF16) for part in parts], axis=1)


def attention(packed, count):
    channels = packed.shape[1] // 3
    head_width = channels // HEADS
    per_group = LANES // head_width
    groups = channels // LANES
    scale = head_width ** (-0.5) * 1.4426950408889634
    lane = lax.broadcasted_iota(jnp.int32, (1, LANES), 1)
    masks = [jnp.where(lane // head_width == h, 1.0, 0.0).astype(BF16) for h in range(per_group)]
    low = lane < PER
    row = lax.broadcasted_iota(jnp.int32, (per_group * PER, LANES), 0)
    col = lax.broadcasted_iota(jnp.int32, (per_group * PER, LANES), 1)
    ones = jnp.where(row // PER == col // head_width, 1.0, 0.0).astype(BF16)

    def piece(kind, w, g):
        start = kind * channels + g * LANES
        return packed[w * PER : (w + 1) * PER, start : start + LANES]

    def by_head(x):
        return jnp.concatenate([x * m for m in masks], axis=0)

    items = [(w, g) for g in range(groups) for w in range(count)]
    scores = [dot_nt(piece(0, w, g), by_head(piece(1, w, g))) for w, g in items]
    weights = []
    for s in scores:
        parts = []
        for p in range(per_group * PER // LANES):
            sp = s[:, p * LANES : (p + 1) * LANES]
            m0 = jnp.max(jnp.where(low, sp, -jnp.inf), axis=-1, keepdims=True)
            m1 = jnp.max(jnp.where(low, -jnp.inf, sp), axis=-1, keepdims=True)
            parts.append(jnp.exp2((sp - jnp.where(low, m0, m1)) * scale).astype(BF16))
        weights.append(jnp.concatenate(parts, axis=1))
    total = dot(jnp.concatenate(weights, axis=0), ones)
    tops = [dot(e, by_head(piece(2, w, g))) for (w, g), e in zip(items, weights)]
    mixed = (jnp.concatenate(tops, axis=0) / total).astype(BF16)
    size = count * PER
    return jnp.concatenate([mixed[g * size : (g + 1) * size] for g in range(groups)], axis=1)


def section(x, flags, attend, merge, expand, reduce_weight):
    count = x.shape[0] // PER

    def gated(base, update, scale=1.0):
        return jnp.concatenate(
            [
                base[w * PER : (w + 1) * PER] + (flags[w] * scale) * update[w * PER : (w + 1) * PER]
                for w in range(count)
            ],
            axis=0,
        )

    packed = dot(layer_norm(x), attend[...]).astype(BF16)
    attended = gated(x, dot(attention(packed, count), merge[...]))
    normed = layer_norm(attended, HALF_ROOT)
    hidden_width = expand.shape[1]
    step = min(256, hidden_width)
    reduced = None
    for start in range(0, hidden_width, step):
        hidden = gelu_scaled(dot(normed, expand[:, start : start + step])).astype(BF16)
        part = dot(hidden, reduce_weight[start : start + step, :])
        reduced = part if reduced is None else reduced + part
    return gated(attended, reduced, HALF_ROOT)


def mbconv(main, above, below, sides, conv_expand, conv_kernel, conv_reduce):
    rows, breadth, channels = main.shape
    inner = (rows + 2) * breadth
    side_rows = sides.shape[0] // 2
    x = jnp.concatenate([above, main, below], axis=0).reshape(inner, channels)
    normed = layer_norm(jnp.concatenate([x, sides], axis=0), HALF_ROOT)
    width = conv_expand.shape[1]
    step = min(256, width)
    taps = conv_kernel[...] * jnp.asarray(0.5, BF16)
    projected = None
    for start in range(0, width, step):
        e = gelu_scaled(dot(normed, conv_expand[:, start : start + step])).astype(BF16)
        body = e[:inner].reshape(rows + 2, breadth, step)
        side = e[inner:].astype(F32)
        sums, edges = [], []
        for j in range(3):
            k = [taps[3 * i + j : 3 * i + j + 1, start : start + step] for i in range(3)]
            total = body[0:rows] * k[0] + body[1 : rows + 1] * k[1] + body[2 : rows + 2] * k[2]
            sums.append(total.astype(F32))
            if j != 1:
                part = side[:side_rows] if j == 0 else side[side_rows:]
                edge = sum(part[i : i + rows] * k[i].astype(F32) for i in range(3))
                edges.append(edge.reshape(rows, 1, step))
        left = jnp.concatenate([edges[0], sums[0][:, : breadth - 1]], axis=1)
        right = jnp.concatenate([sums[2][:, 1:], edges[1]], axis=1)
        spatial = gelu_scaled(sums[1] + left + right)
        spatial = spatial.reshape(rows * breadth, step).astype(BF16)
        part = dot(spatial, conv_reduce[start : start + step, :])
        projected = part if projected is None else projected + part
    return main + projected.reshape(rows, breadth, channels) * HALF_ROOT


def band_kernel(
    first_block,
    direct,
    flags_ref,
    main_ref,
    above_ref,
    below_ref,
    top_ref,
    bottom_ref,
    sides_ref,
    grid_flags_ref,
    conv_expand,
    conv_kernel,
    conv_reduce,
    attend,
    merge,
    expand,
    reduce_weight,
    out_ref,
):
    rows, breadth, channels = main_ref.shape
    bands, per_row = rows // WIN, breadth // WIN
    step = pl.program_id(0)
    first_band = (first_block + step * CHUNKS) * bands
    last_band = flags_ref.shape[0] - bands
    above = jnp.where(first_band == 0, top_ref[...].astype(F32), above_ref[...].astype(F32))
    below = jnp.where(
        first_band == last_band, bottom_ref[...].astype(F32), below_ref[...].astype(F32)
    )
    after = mbconv(
        main_ref[...].astype(F32),
        above,
        below,
        sides_ref[0].astype(F32),
        conv_expand,
        conv_kernel,
        conv_reduce,
    )
    windows = [(t, v) for t in range(bands) for v in range(per_row)]
    x = jnp.concatenate(
        [
            after[t * WIN : (t + 1) * WIN, v * WIN : (v + 1) * WIN].reshape(PER, channels)
            for t, v in windows
        ],
        axis=0,
    )
    flags = [flags_ref[first_band + t, v].astype(F32) for t, v in windows]
    out = section(x, flags, attend, merge, expand, reduce_weight)
    square = {
        tv: out[n * PER : (n + 1) * PER].reshape(WIN, WIN, channels)
        for n, tv in enumerate(windows)
    }
    if direct:
        cols = out_ref.shape[1]
        span = breadth // cols
        for t in range(bands):
            place = step * bands + t
            start = pl.multiple_of(place * span, span)
            for group in range(cols):
                pieces = [square[t, v] for v in range(group, per_row, cols)]
                column = lax.rem(group + 2 * cols - turn(step, t), cols)
                out_ref[:, column, pl.ds(start, span)] = jnp.concatenate(pieces, axis=1).astype(
                    BF16
                )
        used = pl.num_programs(0) * bands * span
        if out_ref.shape[2] > used:
            out_ref[:, :, used:] = jnp.broadcast_to(
                grid_flags_ref[...], out_ref.shape[:2] + grid_flags_ref.shape
            )
    else:
        for t in range(bands):
            pieces = [square[t, v] for v in range(per_row)]
            out_ref[t * WIN : (t + 1) * WIN] = jnp.concatenate(pieces, axis=1).astype(BF16)


def turn(step, t):
    return step + 2 * t


def grid_static_kernel(first_block, flags_ref, x_ref, attend, merge, expand, reduce_weight, out_ref):
    bands = x_ref.shape[0]
    tokens = WIN * PER
    first_band = (first_block + pl.program_id(0) * CHUNKS) * bands
    flags = [flags_ref[first_band + t, w].astype(F32) for t in range(bands) for w in range(WIN)]
    x = jnp.concatenate([x_ref[t].astype(F32) for t in range(bands)], axis=0)
    out = section(x, flags, attend, merge, expand, reduce_weight)
    for t in range(bands):
        out_ref[t] = out[t * tokens : (t + 1) * tokens].astype(BF16)


def grid_live_kernel(mine_ref, x_ref, attend, merge, expand, reduce_weight, out_ref):
    s = pl.program_id(0)
    shape = x_ref.shape
    tokens = WIN * PER

    @pl.when(s < mine_ref[PLACES])
    def _():
        x = x_ref[...].reshape(tokens, shape[-1])
        row = lax.broadcasted_iota(jnp.int32, (tokens, tokens), 0)
        col = lax.broadcasted_iota(jnp.int32, (tokens, tokens), 1)
        order = jnp.where(col == (row % PER) * WIN + row // PER, 1.0, 0.0).astype(BF16)
        back = jnp.where(row == (col % PER) * WIN + col // PER, 1.0, 0.0).astype(BF16)
        base = WIN + mine_ref[s] * WIN
        flags = [mine_ref[base + w].astype(F32) for w in range(WIN)]
        out = section(dot(order, x), flags, attend, merge, expand, reduce_weight)
        out_ref[...] = dot(back, out.astype(BF16)).astype(BF16).reshape(shape)


def plan_kernel(me_ref, flags_ref, slots_ref, lists_ref, mine_ref, most_ref):
    devices = flags_ref.shape[0]
    cols = devices // WIN
    most_ref[0] = 0
    for h in range(CHUNKS):

        def one(d, _, h=h):
            i, c = d // cols, lax.rem(d, cols)
            for s in range(PLACES):
                lists_ref[h, d * PLACES + s] = 0
            count = jnp.int32(0)
            for place in range(PLACES):
                step, t = divmod(place, STEP_BANDS)
                band = (h + step * CHUNKS) * STEP_BANDS + t
                source = band * cols + lax.rem(c + turn(step, t), cols)
                flags = [flags_ref[source, i * WIN + w] for w in range(WIN)]
                live = functools.reduce(jnp.maximum, flags)
                live = jnp.where(live != 0, 1, 0)
                slots_ref[h, place * devices + d] = jnp.where(live == 1, count, -1)
                lists_ref[h, d * PLACES + count] = jnp.where(live == 1, place, 0)

                @pl.when(d == me_ref[0])
                def _(flags=flags, place=place):
                    for w in range(WIN):
                        mine_ref[h, WIN + place * WIN + w] = flags[w]

                count = count + live

            @pl.when(d == me_ref[0])
            def _():
                for s in range(PLACES):
                    mine_ref[h, s] = lists_ref[h, d * PLACES + s]
                mine_ref[h, PLACES] = count

            most_ref[0] = jnp.maximum(most_ref[0], count)
            return 0

        lax.fori_loop(0, devices, one, 0)


def pack_kernel(lists_ref, x_ref, out_ref):
    span = x_ref.shape[1] // PLACES
    slots = out_ref.shape[1] // span

    def one(d, _):
        for s in range(slots):
            start = pl.multiple_of(lists_ref[d * PLACES + s] * span, span)
            out_ref[d, s * span : (s + 1) * span] = x_ref[d, pl.ds(start, span)]
        return 0

    lax.fori_loop(0, x_ref.shape[0], one, 0)


def merge_kernel(slots_ref, back_ref, own_ref, _, out_ref):
    devices = back_ref.shape[0]
    cols = devices // WIN
    span = out_ref.shape[2] // cols
    step = pl.program_id(0)
    for t in range(STEP_BANDS):
        place = step * STEP_BANDS + t
        mine = pl.multiple_of(place * span, span)

        def one(i, _, t=t, place=place, mine=mine):
            blocks = []
            for group in range(cols):
                device = i * cols + lax.rem(group + 2 * cols - turn(step, t), cols)
                slot = slots_ref[place * devices + device]
                start = pl.multiple_of(jnp.maximum(slot, 0) * span, span)
                there = back_ref[device, pl.ds(start, span)].astype(F32)
                here = own_ref[device, pl.ds(mine, span)].astype(F32)
                blocks.append(jnp.where(slot >= 0, there, here))
            pieces = [
                b[h * WIN : (h + 1) * WIN] for h in range(span // WIN) for b in blocks
            ]
            out_ref[0, t * WIN + i] = jnp.concatenate(pieces, axis=0).astype(BF16)
            return 0

        lax.fori_loop(0, WIN, one, 0)


def whole(array):
    return pl.BlockSpec(array.shape, lambda *_: (0,) * array.ndim)


def shift(array, axis, up):
    size = lax.axis_size(axis)
    pairs = [(i, i + 1) for i in range(size - 1)]
    return lax.ppermute(array, axis, pairs if up else [(j, i) for i, j in pairs])


PARAMS = pltpu.CompilerParams(vmem_limit_bytes=60 << 20)


def along(shape, axis, size):
    block = shape[:axis] + (size,) + shape[axis + 1 :]
    return pl.BlockSpec(
        block, lambda i, f: (0,) * axis + (i,) + (0,) * (len(shape) - axis - 1)
    )


def call(kernel, steps, flags, specs, arrays, shape, out_spec, name, aliases={}):
    return pl.pallas_call(
        kernel,
        out_shape=jax.ShapeDtypeStruct(shape, BF16),
        grid_spec=pltpu.PrefetchScalarGridSpec(
            num_scalar_prefetch=1, grid=(steps,), in_specs=specs, out_specs=out_spec
        ),
        compiler_params=PARAMS,
        input_output_aliases=aliases,
        name=name,
    )(flags, *arrays)


def feature_halo(features):
    height, breadth, _ = features.shape
    top = shift(features[height - 1 :], "row", True)
    bottom = shift(features[:1], "row", False)
    edge_columns = [
        jnp.concatenate([top[:, c], features[:, c], bottom[:, c]], axis=0) for c in (0, breadth - 1)
    ]
    left = shift(edge_columns[1], "col", True)
    right = shift(edge_columns[0], "col", False)
    return top, bottom, left, right


def exchange(array):
    return lax.all_to_all(array, ("row", "col"), split_axis=0, concat_axis=0, tiled=True)


def on_device(
    features,
    conv_expand,
    conv_kernel,
    conv_reduce,
    block_attend,
    block_merge,
    block_expand,
    block_reduce,
    grid_attend,
    grid_merge,
    grid_expand,
    grid_reduce,
    block_valid,
    grid_valid,
):
    height, breadth, channels = features.shape
    rows, cols = lax.axis_size("row"), lax.axis_size("col")
    devices = rows * cols
    parity = rows // GRID
    direct = parity == 1 and breadth % (2 * WIN * cols) == 0
    step_rows = STEP_BANDS * WIN
    steps = height // step_rows // CHUNKS
    per_chunk = steps * STEP_BANDS
    direct = direct and per_chunk == PLACES
    conv_weights = (conv_expand, conv_kernel, conv_reduce)
    block_weights = (block_attend, block_merge, block_expand, block_reduce)
    grid_weights = (grid_attend, grid_merge, grid_expand, grid_reduce)

    top, bottom, left, right = feature_halo(features)
    padded = -(-(step_rows + 2) // 8) * 8
    gap = jnp.zeros((padded - step_rows - 2, channels), BF16)
    sides = jnp.stack(
        [
            jnp.concatenate([left[r : r + step_rows + 2], gap, right[r : r + step_rows + 2], gap])
            for r in range(0, height, step_rows)
        ]
    )
    flag_row = jnp.pad(grid_valid.reshape(1, -1).astype(BF16), ((0, 7), (0, channels - WIN * WIN)))
    row_block = (1, breadth, channels)

    def blocks_of(h):
        arrays = [features, features, features, top, bottom, sides, flag_row]
        arrays += [*conv_weights, *block_weights]

        def row_at(offset):
            def index(i, f):
                row = (h + i * CHUNKS) * step_rows + offset
                return jnp.clip(row, 0, height - 1), 0, 0

            return pl.BlockSpec(row_block, index)

        specs = [
            pl.BlockSpec((step_rows, breadth, channels), lambda i, f: (h + i * CHUNKS, 0, 0)),
            row_at(-1),
            row_at(step_rows),
            whole(top),
            whole(bottom),
            pl.BlockSpec((1, *sides.shape[1:]), lambda i, f: (h + i * CHUNKS, 0, 0)),
        ] + [whole(a) for a in arrays[6:]]
        if direct:
            extra = flag_row.shape[0] if h == 0 else 0
            shape = (rows, cols, per_chunk * (breadth // cols) + extra, channels)
            out_spec = pl.BlockSpec(shape, lambda i, f: (0, 0, 0, 0))
        else:
            shape = (steps * step_rows, breadth, channels)
            out_spec = along(shape, 0, step_rows)
        kernel = functools.partial(band_kernel, h, direct)
        return call(kernel, steps, block_valid, specs, arrays, shape, out_spec, "conv_and_blocks")

    if direct:
        return live_groups(blocks_of, grid_weights, (height, breadth, channels), rows, cols)

    repeat = breadth // (WIN * cols)
    part = WIN // parity
    me = lax.axis_index("row")
    flags = grid_valid[:, :, 0, :]
    spread = exchange(jnp.broadcast_to(flags[None], (devices, *flags.shape)))
    spread = spread.reshape(rows, cols, *flags.shape)
    spread = lax.dynamic_index_in_dim(spread, lax.axis_index("col"), 1, keepdims=False)
    by_band = jnp.transpose(spread, (1, 0, 2, 3)).reshape(parity, height // WIN, WIN, WIN)
    mine = lax.dynamic_index_in_dim(by_band, me // parity, 2, keepdims=False)
    mine = lax.dynamic_slice_in_dim(mine, (me % parity) * part, part, 2)
    grid_flags = jnp.transpose(mine, (1, 0, 2)).reshape(height // WIN, WIN)
    outputs = []
    for h in range(CHUNKS):
        split = blocks_of(h).reshape(per_chunk, WIN, repeat, cols, parity, part, channels)
        sending = jnp.transpose(split, (1, 4, 3, 0, 2, 5, 6))
        arrived = exchange(sending.reshape(devices, per_chunk, repeat * part, channels))
        split = arrived.reshape(GRID, parity, cols, per_chunk, repeat, part, channels)
        arrived = jnp.transpose(split, (3, 1, 5, 0, 2, 4, 6))
        arrived = arrived.reshape(per_chunk, WIN * PER, channels)
        spec = along(arrived.shape, 0, STEP_BANDS)
        finished = call(
            functools.partial(grid_static_kernel, h),
            steps,
            grid_flags,
            [spec] + [whole(a) for a in grid_weights],
            [arrived, *grid_weights],
            arrived.shape,
            spec,
            "grid_section",
        )
        split = finished.reshape(per_chunk, parity, part, GRID, cols, repeat, channels)
        finished = jnp.transpose(split, (3, 1, 4, 0, 5, 2, 6))
        returned = exchange(finished.reshape(devices, per_chunk, repeat * part, channels))
        split = returned.reshape(WIN, parity, cols, per_chunk, repeat, part, channels)
        spread = jnp.transpose(split, (3, 0, 4, 2, 1, 5, 6))
        outputs.append(spread.reshape(steps, step_rows, breadth, channels))
    return jnp.stack(outputs, axis=1).reshape(height, breadth, channels)


def live_groups(blocks_of, grid_weights, tile, rows, cols):
    height, breadth, channels = tile
    devices = rows * cols
    span = breadth // cols
    step_rows = STEP_BANDS * WIN
    steps = PLACES // STEP_BANDS
    smem = pl.BlockSpec(memory_space=pltpu.SMEM)
    first = blocks_of(0).reshape(devices, -1, channels)
    arrived = exchange(first)
    second = blocks_of(1).reshape(devices, -1, channels)
    flags = arrived[:, PLACES * span, : WIN * WIN].astype(jnp.int32)
    me = (lax.axis_index("row") * cols + lax.axis_index("col")).reshape(1)
    table = jax.ShapeDtypeStruct((CHUNKS, PLACES * devices), jnp.int32)
    slots, lists, mine, most = pl.pallas_call(
        plan_kernel,
        out_shape=(
            table,
            table,
            jax.ShapeDtypeStruct((CHUNKS, WIN + PLACES * WIN), jnp.int32),
            jax.ShapeDtypeStruct((1,), jnp.int32),
        ),
        in_specs=[smem, smem],
        out_specs=(smem,) * 4,
        name="plan",
    )(me, flags)

    def branch(count):
        shape = (devices, count * span, channels)
        block = (devices, span, channels)
        by_slot = pl.BlockSpec(block, lambda s, m: (0, s, 0))
        by_place = pl.BlockSpec(block, lambda s, m: (0, m[s], 0))

        def sections(h, x, spec, mine, weights):
            arrays = [x, *weights]
            specs = [spec] + [whole(a) for a in weights]
            return call(
                grid_live_kernel, count, mine[h], specs, arrays, shape, by_slot, "grid_section"
            )

        def merged(h, slots, back, own, base):
            out_shape = (CHUNKS * steps, step_rows, breadth, channels)
            out_spec = pl.BlockSpec(
                (1, *out_shape[1:]), lambda i, f: (h + i * CHUNKS, 0, 0, 0)
            )
            specs = [whole(back), whole(own), pl.BlockSpec(memory_space=pl.ANY)]
            return call(
                merge_kernel, steps, slots[h], specs, [back, own, base], out_shape, out_spec,
                "merge", {} if h == 0 else {3: 0},
            )

        def run(first, arrived, second, slots, lists, mine, *weights):
            packed = call(
                pack_kernel, 1, lists[1], [whole(second)], [second], shape,
                pl.BlockSpec(shape, lambda i, f: (0, 0, 0)), "pack",
            )
            other = exchange(packed)
            back = exchange(sections(0, arrived, by_place, mine, weights))
            other = exchange(sections(1, other, by_slot, mine, weights))
            out = merged(0, slots, back, first, back)
            return merged(1, slots, other, second, out)

        return run

    index = jnp.clip(most[0], 1, PLACES) - 1
    out = lax.switch(
        index,
        [branch(n + 1) for n in range(PLACES)],
        first, arrived, second, slots, lists, mine, *grid_weights,
    )
    return out.reshape(height, breadth, channels)


def solution(mesh):
    in_specs = (P("row", "col", None),) + (P(),) * 11
    in_specs += (P("row", "col"), P(None, "row", None, "col"))
    return jax.shard_map(
        on_device,
        mesh=mesh,
        in_specs=in_specs,
        out_specs=P("row", "col", None),
        check_vma=False,
    )
```

```python
import functools

import jax
import jax.numpy as jnp
from jax import lax
from jax.experimental import pallas as pl
from jax.experimental.pallas import tpu as pltpu
from jax.sharding import PartitionSpec as P

HEADS = 8
WIN = 8
GRID = 8
PER = 64
EPSILON = 1e-05
LANES = 128
F32 = jnp.float32
BF16 = jnp.bfloat16
CHUNKS = 2
STEP_BANDS = 2
PLACES = 4
PART = 4
SIZES = ((2, 1), (3, 2), (3, 3), (4, 4))


def dot(a, b):
    return jnp.dot(a, b, preferred_element_type=F32)


def dot_nt(a, b):
    return lax.dot_general(a, b, (((1,), (1,)), ((), ())), preferred_element_type=F32)


HALF_ROOT = 0.7071067811865476


def gelu_scaled(y):
    return y + y * lax.erf(y)


def layer_norm(x, scale=1.0):
    channels = x.shape[1]
    average = jnp.full((channels, LANES), 1.0 / channels, BF16)
    rounded = x.astype(BF16)
    mean = dot(rounded, average)
    wide = rounded.astype(F32)
    parts = [wide[:, s : s + LANES] - mean for s in range(0, channels, LANES)]
    squares = jnp.concatenate([(part * part).astype(BF16) for part in parts], axis=1)
    factor = lax.rsqrt(dot(squares, average) + EPSILON) * scale
    return jnp.concatenate([(part * factor).astype(BF16) for part in parts], axis=1)


def attention(packed, count):
    channels = packed.shape[1] // 3
    head_width = channels // HEADS
    per_group = LANES // head_width
    groups = channels // LANES
    scale = head_width ** (-0.5) * 1.4426950408889634
    lane = lax.broadcasted_iota(jnp.int32, (1, LANES), 1)
    masks = [jnp.where(lane // head_width == h, 1.0, 0.0).astype(BF16) for h in range(per_group)]
    low = lane < PER
    row = lax.broadcasted_iota(jnp.int32, (per_group * PER, LANES), 0)
    col = lax.broadcasted_iota(jnp.int32, (per_group * PER, LANES), 1)
    ones = jnp.where(row // PER == col // head_width, 1.0, 0.0).astype(BF16)

    def piece(kind, w, g):
        start = kind * channels + g * LANES
        return packed[w * PER : (w + 1) * PER, start : start + LANES]

    def by_head(x):
        return jnp.concatenate([x * m for m in masks], axis=0)

    items = [(w, g) for g in range(groups) for w in range(count)]
    scores = [dot_nt(piece(0, w, g), by_head(piece(1, w, g))) for w, g in items]
    weights = []
    for s in scores:
        parts = []
        for p in range(per_group * PER // LANES):
            sp = s[:, p * LANES : (p + 1) * LANES]
            m0 = jnp.max(jnp.where(low, sp, -jnp.inf), axis=-1, keepdims=True)
            m1 = jnp.max(jnp.where(low, -jnp.inf, sp), axis=-1, keepdims=True)
            parts.append(jnp.exp2((sp - jnp.where(low, m0, m1)) * scale).astype(BF16))
        weights.append(jnp.concatenate(parts, axis=1))
    total = dot(jnp.concatenate(weights, axis=0), ones)
    tops = [dot(e, by_head(piece(2, w, g))) for (w, g), e in zip(items, weights)]
    mixed = (jnp.concatenate(tops, axis=0) / total).astype(BF16)
    size = count * PER
    return jnp.concatenate([mixed[g * size : (g + 1) * size] for g in range(groups)], axis=1)


def section(x, flags, attend, merge, expand, reduce_weight):
    count = x.shape[0] // PER

    def gated(base, update, scale=1.0):
        return jnp.concatenate(
            [
                base[w * PER : (w + 1) * PER] + (flags[w] * scale) * update[w * PER : (w + 1) * PER]
                for w in range(count)
            ],
            axis=0,
        )

    packed = dot(layer_norm(x), attend[...]).astype(BF16)
    attended = gated(x, dot(attention(packed, count), merge[...]))
    normed = layer_norm(attended, HALF_ROOT)
    hidden_width = expand.shape[1]
    step = min(256, hidden_width)
    reduced = None
    for start in range(0, hidden_width, step):
        hidden = gelu_scaled(dot(normed, expand[:, start : start + step])).astype(BF16)
        part = dot(hidden, reduce_weight[start : start + step, :])
        reduced = part if reduced is None else reduced + part
    return gated(attended, reduced, HALF_ROOT)


def mbconv(main, above, below, sides, conv_expand, conv_kernel, conv_reduce):
    rows, breadth, channels = main.shape
    inner = (rows + 2) * breadth
    side_rows = sides.shape[0] // 2
    x = jnp.concatenate([above, main, below], axis=0).reshape(inner, channels)
    normed = layer_norm(jnp.concatenate([x, sides], axis=0), HALF_ROOT)
    width = conv_expand.shape[1]
    step = min(256, width)
    taps = conv_kernel[...] * jnp.asarray(0.5, BF16)
    projected = None
    for start in range(0, width, step):
        e = gelu_scaled(dot(normed, conv_expand[:, start : start + step])).astype(BF16)
        body = e[:inner].reshape(rows + 2, breadth, step)
        side = e[inner:].astype(F32)
        sums, edges = [], []
        for j in range(3):
            k = [taps[3 * i + j : 3 * i + j + 1, start : start + step] for i in range(3)]
            total = body[0:rows] * k[0] + body[1 : rows + 1] * k[1] + body[2 : rows + 2] * k[2]
            sums.append(total.astype(F32))
            if j != 1:
                part = side[:side_rows] if j == 0 else side[side_rows:]
                edge = sum(part[i : i + rows] * k[i].astype(F32) for i in range(3))
                edges.append(edge.reshape(rows, 1, step))
        left = jnp.concatenate([edges[0], sums[0][:, : breadth - 1]], axis=1)
        right = jnp.concatenate([sums[2][:, 1:], edges[1]], axis=1)
        spatial = gelu_scaled(sums[1] + left + right)
        spatial = spatial.reshape(rows * breadth, step).astype(BF16)
        part = dot(spatial, conv_reduce[start : start + step, :])
        projected = part if projected is None else projected + part
    return main + projected.reshape(rows, breadth, channels) * HALF_ROOT


def band_kernel(
    first_block,
    direct,
    flags_ref,
    main_ref,
    above_ref,
    below_ref,
    top_ref,
    bottom_ref,
    sides_ref,
    grid_flags_ref,
    conv_expand,
    conv_kernel,
    conv_reduce,
    attend,
    merge,
    expand,
    reduce_weight,
    out_ref,
):
    rows, breadth, channels = main_ref.shape
    bands, per_row = rows // WIN, breadth // WIN
    step = pl.program_id(0)
    first_band = (first_block + step * CHUNKS) * bands
    last_band = flags_ref.shape[0] - bands
    above = jnp.where(first_band == 0, top_ref[...].astype(F32), above_ref[...].astype(F32))
    below = jnp.where(
        first_band == last_band, bottom_ref[...].astype(F32), below_ref[...].astype(F32)
    )
    after = mbconv(
        main_ref[...].astype(F32),
        above,
        below,
        sides_ref[0].astype(F32),
        conv_expand,
        conv_kernel,
        conv_reduce,
    )
    windows = [(t, v) for t in range(bands) for v in range(per_row)]
    x = jnp.concatenate(
        [
            after[t * WIN : (t + 1) * WIN, v * WIN : (v + 1) * WIN].reshape(PER, channels)
            for t, v in windows
        ],
        axis=0,
    )
    flags = [flags_ref[first_band + t, v].astype(F32) for t, v in windows]
    out = section(x, flags, attend, merge, expand, reduce_weight)
    square = {
        tv: out[n * PER : (n + 1) * PER].reshape(WIN, WIN, channels)
        for n, tv in enumerate(windows)
    }
    if direct:
        cols = out_ref.shape[1]
        span = breadth // cols
        for t in range(bands):
            place = step * bands + t
            start = pl.multiple_of(place * span, span)
            for group in range(cols):
                pieces = [square[t, v] for v in range(group, per_row, cols)]
                column = lax.rem(group + 2 * cols - turn(step, t), cols)
                out_ref[:, column, pl.ds(start, span)] = jnp.concatenate(pieces, axis=1).astype(
                    BF16
                )
        used = pl.num_programs(0) * bands * span
        if out_ref.shape[2] > used:
            out_ref[:, :, used:] = jnp.broadcast_to(
                grid_flags_ref[...], out_ref.shape[:2] + grid_flags_ref.shape
            )
    else:
        for t in range(bands):
            pieces = [square[t, v] for v in range(per_row)]
            out_ref[t * WIN : (t + 1) * WIN] = jnp.concatenate(pieces, axis=1).astype(BF16)


def turn(step, t):
    return step + 2 * t


def grid_static_kernel(first_block, flags_ref, x_ref, attend, merge, expand, reduce_weight, out_ref):
    bands = x_ref.shape[0]
    tokens = WIN * PER
    first_band = (first_block + pl.program_id(0) * CHUNKS) * bands
    flags = [flags_ref[first_band + t, w].astype(F32) for t in range(bands) for w in range(WIN)]
    x = jnp.concatenate([x_ref[t].astype(F32) for t in range(bands)], axis=0)
    out = section(x, flags, attend, merge, expand, reduce_weight)
    for t in range(bands):
        out_ref[t] = out[t * tokens : (t + 1) * tokens].astype(BF16)


def grid_live_kernel(
    mine_ref, x_ref, attend, merge, expand, reduce_weight, out_ref, in_ref, done_ref
):
    s = pl.program_id(0)
    shape = x_ref.shape
    tokens = WIN * PER

    @pl.when(s < mine_ref[PLACES])
    def _():
        x = x_ref[...].astype(F32).reshape(tokens, shape[-1])
        halves = range(shape[-1] // LANES)
        for n in halves:
            in_ref[n] = x[:, n * LANES : (n + 1) * LANES]
        base = WIN + mine_ref[s] * WIN

        def part(n, _):
            windows = [n * PART + w for w in range(PART)]
            spots = [pl.ds(w, PER, stride=WIN) for w in windows]
            x = jnp.concatenate(
                [jnp.concatenate([in_ref[n, spot] for n in halves], axis=1) for spot in spots],
                axis=0,
            )
            flags = [mine_ref[base + w].astype(F32) for w in windows]
            out = section(x, flags, attend, merge, expand, reduce_weight)
            for w, spot in enumerate(spots):
                for n in halves:
                    done_ref[n, spot] = out[
                        w * PER : (w + 1) * PER, n * LANES : (n + 1) * LANES
                    ]
            return 0

        lax.fori_loop(0, WIN // PART, part, 0)
        out = jnp.concatenate([done_ref[n] for n in halves], axis=1)
        out_ref[...] = out.astype(BF16).reshape(shape)


def plan_kernel(
    me_ref, flags_ref, live_ref, slots0_ref, slots1_ref, lists_ref, mine0_ref, mine1_ref, size_ref
):
    devices = flags_ref.shape[0]
    cols = devices // WIN
    me = me_ref[0]

    def source(h, place, c):
        step, t = divmod(place, STEP_BANDS)
        band = (h + step * CHUNKS) * STEP_BANDS + t
        return band * cols + lax.rem(c + turn(step, t), cols)

    most = []
    for h, slots_ref, mine_ref in ((0, slots0_ref, mine0_ref), (1, slots1_ref, mine1_ref)):

        def one(d, top, h=h, slots_ref=slots_ref):
            i, c = d // cols, lax.rem(d, cols)
            count = jnp.int32(0)
            for place in range(PLACES):
                live = live_ref[source(h, place, c), i] != 0
                slots_ref[place * devices + d] = jnp.where(live, count, -1)
                if h == 1:
                    lists_ref[d * PLACES + place] = 0
                    lists_ref[d * PLACES + count] = jnp.where(live, place, 0)
                count = count + jnp.where(live, 1, 0)
            return jnp.maximum(top, count)

        most.append(lax.fori_loop(0, devices, one, jnp.int32(0)))
        row, column = me // cols, lax.rem(me, cols)
        count = jnp.int32(0)
        for place in range(PLACES):
            at = source(h, place, column)
            live = live_ref[at, row] != 0
            mine_ref[place] = 0
            mine_ref[count] = jnp.where(live, place, 0)
            count = count + jnp.where(live, 1, 0)
            for w in range(WIN):
                mine_ref[WIN + place * WIN + w] = flags_ref[at, row * WIN + w]
        mine_ref[PLACES] = count
    size = jnp.int32(len(SIZES) - 1)
    for n in reversed(range(len(SIZES) - 1)):
        fits = (most[0] <= SIZES[n][0]) & (most[1] <= SIZES[n][1])
        size = jnp.where(fits, n, size)
    size_ref[0] = size


def pack_kernel(lists_ref, x_ref, out_ref):
    span = x_ref.shape[1] // PLACES
    slots = out_ref.shape[1] // span

    def one(d, _):
        for s in range(slots):
            start = pl.multiple_of(lists_ref[d * PLACES + s] * span, span)
            out_ref[d, s * span : (s + 1) * span] = x_ref[d, pl.ds(start, span)]
        return 0

    lax.fori_loop(0, x_ref.shape[0], one, 0, unroll=4)


def merge_kernel(slots_ref, back_ref, own_ref, _, out_ref):
    devices = back_ref.shape[0]
    cols = devices // WIN
    span = out_ref.shape[2] // cols
    step = pl.program_id(0)
    for t in range(STEP_BANDS):
        place = step * STEP_BANDS + t
        mine = pl.multiple_of(place * span, span)

        def one(i, _, t=t, place=place, mine=mine):
            blocks = []
            for group in range(cols):
                device = i * cols + lax.rem(group + 2 * cols - turn(step, t), cols)
                slot = slots_ref[place * devices + device]
                start = pl.multiple_of(jnp.maximum(slot, 0) * span, span)
                there = back_ref[device, pl.ds(start, span)].astype(F32)
                here = own_ref[device, pl.ds(mine, span)].astype(F32)
                blocks.append(jnp.where(slot >= 0, there, here))
            pieces = [
                b[h * WIN : (h + 1) * WIN] for h in range(span // WIN) for b in blocks
            ]
            out_ref[0, t * WIN + i] = jnp.concatenate(pieces, axis=0).astype(BF16)
            return 0

        lax.fori_loop(0, WIN, one, 0, unroll=2)


def whole(array):
    return pl.BlockSpec(array.shape, lambda *_: (0,) * array.ndim)


def shift(array, axis, up):
    size = lax.axis_size(axis)
    pairs = [(i, i + 1) for i in range(size - 1)]
    return lax.ppermute(array, axis, pairs if up else [(j, i) for i, j in pairs])


PARAMS = pltpu.CompilerParams(vmem_limit_bytes=60 << 20)


def along(shape, axis, size):
    block = shape[:axis] + (size,) + shape[axis + 1 :]
    return pl.BlockSpec(
        block, lambda i, f: (0,) * axis + (i,) + (0,) * (len(shape) - axis - 1)
    )


def call(kernel, steps, flags, specs, arrays, shape, out_spec, name, aliases={}, scratch=()):
    return pl.pallas_call(
        kernel,
        out_shape=jax.ShapeDtypeStruct(shape, BF16),
        grid_spec=pltpu.PrefetchScalarGridSpec(
            num_scalar_prefetch=1, grid=(steps,), in_specs=specs, out_specs=out_spec,
            scratch_shapes=scratch,
        ),
        compiler_params=PARAMS,
        input_output_aliases=aliases,
        name=name,
    )(flags, *arrays)


def feature_halo(features):
    height, breadth, _ = features.shape
    top = shift(features[height - 1 :], "row", True)
    bottom = shift(features[:1], "row", False)
    edge_columns = [
        jnp.concatenate([top[:, c], features[:, c], bottom[:, c]], axis=0) for c in (0, breadth - 1)
    ]
    left = shift(edge_columns[1], "col", True)
    right = shift(edge_columns[0], "col", False)
    return top, bottom, left, right


def exchange(array):
    return lax.all_to_all(array, ("row", "col"), split_axis=0, concat_axis=0, tiled=True)


def on_device(
    features,
    conv_expand,
    conv_kernel,
    conv_reduce,
    block_attend,
    block_merge,
    block_expand,
    block_reduce,
    grid_attend,
    grid_merge,
    grid_expand,
    grid_reduce,
    block_valid,
    grid_valid,
):
    height, breadth, channels = features.shape
    rows, cols = lax.axis_size("row"), lax.axis_size("col")
    devices = rows * cols
    parity = rows // GRID
    direct = parity == 1 and breadth % (2 * WIN * cols) == 0
    step_rows = STEP_BANDS * WIN
    steps = height // step_rows // CHUNKS
    per_chunk = steps * STEP_BANDS
    direct = direct and per_chunk == PLACES
    conv_weights = (conv_expand, conv_kernel, conv_reduce)
    block_weights = (block_attend, block_merge, block_expand, block_reduce)
    grid_weights = (grid_attend, grid_merge, grid_expand, grid_reduce)

    top, bottom, left, right = feature_halo(features)
    padded = -(-(step_rows + 2) // 8) * 8
    gap = jnp.zeros((padded - step_rows - 2, channels), BF16)
    sides = jnp.stack(
        [
            jnp.concatenate([left[r : r + step_rows + 2], gap, right[r : r + step_rows + 2], gap])
            for r in range(0, height, step_rows)
        ]
    )
    flag_row = jnp.pad(grid_valid.reshape(1, -1).astype(BF16), ((0, 7), (0, channels - WIN * WIN)))
    row_block = (1, breadth, channels)

    def blocks_of(h):
        arrays = [features, features, features, top, bottom, sides, flag_row]
        arrays += [*conv_weights, *block_weights]

        def row_at(offset):
            def index(i, f):
                row = (h + i * CHUNKS) * step_rows + offset
                return jnp.clip(row, 0, height - 1), 0, 0

            return pl.BlockSpec(row_block, index)

        specs = [
            pl.BlockSpec((step_rows, breadth, channels), lambda i, f: (h + i * CHUNKS, 0, 0)),
            row_at(-1),
            row_at(step_rows),
            whole(top),
            whole(bottom),
            pl.BlockSpec((1, *sides.shape[1:]), lambda i, f: (h + i * CHUNKS, 0, 0)),
        ] + [whole(a) for a in arrays[6:]]
        if direct:
            extra = flag_row.shape[0] if h == 0 else 0
            shape = (rows, cols, per_chunk * (breadth // cols) + extra, channels)
            out_spec = pl.BlockSpec(shape, lambda i, f: (0, 0, 0, 0))
        else:
            shape = (steps * step_rows, breadth, channels)
            out_spec = along(shape, 0, step_rows)
        kernel = functools.partial(band_kernel, h, direct)
        return call(kernel, steps, block_valid, specs, arrays, shape, out_spec, "conv_and_blocks")

    if direct:
        return live_groups(blocks_of, grid_weights, (height, breadth, channels), rows, cols)

    repeat = breadth // (WIN * cols)
    part = WIN // parity
    me = lax.axis_index("row")
    flags = grid_valid[:, :, 0, :]
    spread = exchange(jnp.broadcast_to(flags[None], (devices, *flags.shape)))
    spread = spread.reshape(rows, cols, *flags.shape)
    spread = lax.dynamic_index_in_dim(spread, lax.axis_index("col"), 1, keepdims=False)
    by_band = jnp.transpose(spread, (1, 0, 2, 3)).reshape(parity, height // WIN, WIN, WIN)
    mine = lax.dynamic_index_in_dim(by_band, me // parity, 2, keepdims=False)
    mine = lax.dynamic_slice_in_dim(mine, (me % parity) * part, part, 2)
    grid_flags = jnp.transpose(mine, (1, 0, 2)).reshape(height // WIN, WIN)
    outputs = []
    for h in range(CHUNKS):
        split = blocks_of(h).reshape(per_chunk, WIN, repeat, cols, parity, part, channels)
        sending = jnp.transpose(split, (1, 4, 3, 0, 2, 5, 6))
        arrived = exchange(sending.reshape(devices, per_chunk, repeat * part, channels))
        split = arrived.reshape(GRID, parity, cols, per_chunk, repeat, part, channels)
        arrived = jnp.transpose(split, (3, 1, 5, 0, 2, 4, 6))
        arrived = arrived.reshape(per_chunk, WIN * PER, channels)
        spec = along(arrived.shape, 0, STEP_BANDS)
        finished = call(
            functools.partial(grid_static_kernel, h),
            steps,
            grid_flags,
            [spec] + [whole(a) for a in grid_weights],
            [arrived, *grid_weights],
            arrived.shape,
            spec,
            "grid_section",
        )
        split = finished.reshape(per_chunk, parity, part, GRID, cols, repeat, channels)
        finished = jnp.transpose(split, (3, 1, 4, 0, 5, 2, 6))
        returned = exchange(finished.reshape(devices, per_chunk, repeat * part, channels))
        split = returned.reshape(WIN, parity, cols, per_chunk, repeat, part, channels)
        spread = jnp.transpose(split, (3, 0, 4, 2, 1, 5, 6))
        outputs.append(spread.reshape(steps, step_rows, breadth, channels))
    return jnp.stack(outputs, axis=1).reshape(height, breadth, channels)


def live_groups(blocks_of, grid_weights, tile, rows, cols):
    height, breadth, channels = tile
    devices = rows * cols
    span = breadth // cols
    step_rows = STEP_BANDS * WIN
    steps = PLACES // STEP_BANDS
    smem = pl.BlockSpec(memory_space=pltpu.SMEM)
    first = blocks_of(0).reshape(devices, -1, channels)
    arrived = exchange(first)
    second = blocks_of(1).reshape(devices, -1, channels)
    flags = arrived[:, PLACES * span, : WIN * WIN].astype(jnp.int32)
    live = jnp.max(flags.reshape(devices, WIN, WIN), axis=2)
    me = (lax.axis_index("row") * cols + lax.axis_index("col")).reshape(1)
    table = jax.ShapeDtypeStruct((PLACES * devices,), jnp.int32)
    own = jax.ShapeDtypeStruct((WIN + PLACES * WIN,), jnp.int32)
    *plan, size = pl.pallas_call(
        plan_kernel,
        out_shape=(table, table, table, own, own, jax.ShapeDtypeStruct((1,), jnp.int32)),
        in_specs=[smem] * 3,
        out_specs=(smem,) * 6,
        name="plan",
    )(me, flags, live)

    def branch(counts):
        block = (devices, span, channels)
        by_slot = pl.BlockSpec(block, lambda s, m: (0, s, 0))
        by_place = pl.BlockSpec(block, lambda s, m: (0, m[s], 0))
        shapes = [(devices, count * span, channels) for count in counts]

        def sections(h, x, spec, mine, weights):
            arrays = [x, *weights]
            specs = [spec] + [whole(a) for a in weights]
            return call(
                grid_live_kernel, counts[h], mine, specs, arrays, shapes[h], by_slot,
                "grid_section",
                scratch=(
                    pltpu.VMEM((channels // LANES, WIN * PER, LANES), F32),
                    pltpu.VMEM((channels // LANES, WIN * PER, LANES), F32),
                ),
            )

        def merged(h, slots, back, own, base):
            out_shape = (CHUNKS * steps, step_rows, breadth, channels)
            out_spec = pl.BlockSpec(
                (1, *out_shape[1:]), lambda i, f: (h + i * CHUNKS, 0, 0, 0)
            )
            specs = [whole(back), whole(own), pl.BlockSpec(memory_space=pl.ANY)]
            return call(
                merge_kernel, steps, slots, specs, [back, own, base], out_shape, out_spec,
                "merge", {} if h == 0 else {3: 0},
            )

        def run(first, arrived, second, slots0, slots1, lists, mine0, mine1, *weights):
            packed = call(
                pack_kernel, 1, lists, [whole(second)], [second], shapes[1],
                pl.BlockSpec(shapes[1], lambda i, f: (0, 0, 0)), "pack",
            )
            other = exchange(packed)
            back = exchange(sections(0, arrived, by_place, mine0, weights))
            other = exchange(sections(1, other, by_slot, mine1, weights))
            out = merged(0, slots0, back, first, back)
            return merged(1, slots1, other, second, out)

        return run

    out = lax.switch(
        size[0], [branch(counts) for counts in SIZES], first, arrived, second, *plan, *grid_weights
    )
    return out.reshape(height, breadth, channels)


def solution(mesh):
    in_specs = (P("row", "col", None),) + (P(),) * 11
    in_specs += (P("row", "col"), P(None, "row", None, "col"))
    return jax.shard_map(
        on_device,
        mesh=mesh,
        in_specs=in_specs,
        out_specs=P("row", "col", None),
        check_vma=False,
    )
```

```python
import functools

import jax
import jax.numpy as jnp
from jax import lax
from jax.experimental import pallas as pl
from jax.experimental.pallas import tpu as pltpu
from jax.sharding import PartitionSpec as P

HEADS = 8
WIN = 8
GRID = 8
PER = 64
EPSILON = 1e-05
LANES = 128
F32 = jnp.float32
BF16 = jnp.bfloat16
CHUNKS = 2
STEP_BANDS = 2
PLACES = 4
PART = 4
SIZES = ((2, 1), (3, 2), (3, 3), (4, 4))


def dot(a, b):
    return jnp.dot(a, b, preferred_element_type=F32)


def dot_nt(a, b):
    return lax.dot_general(a, b, (((1,), (1,)), ((), ())), preferred_element_type=F32)


HALF_ROOT = 0.7071067811865476


def gelu_scaled(y):
    return y + y * lax.erf(y)


def layer_norm(x, scale=1.0):
    channels = x.shape[1]
    average = jnp.full((channels, LANES), 1.0 / channels, BF16)
    rounded = x.astype(BF16)
    mean = dot(rounded, average)
    wide = rounded.astype(F32)
    parts = [wide[:, s : s + LANES] - mean for s in range(0, channels, LANES)]
    squares = jnp.concatenate([(part * part).astype(BF16) for part in parts], axis=1)
    factor = lax.rsqrt(dot(squares, average) + EPSILON) * scale
    return jnp.concatenate([(part * factor).astype(BF16) for part in parts], axis=1)


def attention(packed, count):
    channels = packed.shape[1] // 3
    head_width = channels // HEADS
    per_group = LANES // head_width
    groups = channels // LANES
    scale = head_width ** (-0.5) * 1.4426950408889634
    lane = lax.broadcasted_iota(jnp.int32, (1, LANES), 1)
    masks = [jnp.where(lane // head_width == h, 1.0, 0.0).astype(BF16) for h in range(per_group)]
    low = lane < PER
    row = lax.broadcasted_iota(jnp.int32, (per_group * PER, LANES), 0)
    col = lax.broadcasted_iota(jnp.int32, (per_group * PER, LANES), 1)
    ones = jnp.where(row // PER == col // head_width, 1.0, 0.0).astype(BF16)

    def piece(kind, w, g):
        start = kind * channels + g * LANES
        return packed[w * PER : (w + 1) * PER, start : start + LANES]

    def by_head(x):
        return jnp.concatenate([x * m for m in masks], axis=0)

    items = [(w, g) for g in range(groups) for w in range(count)]
    scores = [dot_nt(piece(0, w, g), by_head(piece(1, w, g))) for w, g in items]
    weights = []
    for s in scores:
        parts = []
        for p in range(per_group * PER // LANES):
            sp = s[:, p * LANES : (p + 1) * LANES]
            m0 = jnp.max(jnp.where(low, sp, -jnp.inf), axis=-1, keepdims=True)
            m1 = jnp.max(jnp.where(low, -jnp.inf, sp), axis=-1, keepdims=True)
            parts.append(jnp.exp2((sp - jnp.where(low, m0, m1)) * scale).astype(BF16))
        weights.append(jnp.concatenate(parts, axis=1))
    total = dot(jnp.concatenate(weights, axis=0), ones)
    tops = [dot(e, by_head(piece(2, w, g))) for (w, g), e in zip(items, weights)]
    mixed = (jnp.concatenate(tops, axis=0) / total).astype(BF16)
    size = count * PER
    return jnp.concatenate([mixed[g * size : (g + 1) * size] for g in range(groups)], axis=1)


def section(x, flags, attend, merge, expand, reduce_weight):
    count = x.shape[0] // PER

    def gated(base, update, scale=1.0):
        return jnp.concatenate(
            [
                base[w * PER : (w + 1) * PER] + (flags[w] * scale) * update[w * PER : (w + 1) * PER]
                for w in range(count)
            ],
            axis=0,
        )

    packed = dot(layer_norm(x), attend[...]).astype(BF16)
    attended = gated(x, dot(attention(packed, count), merge[...]))
    normed = layer_norm(attended, HALF_ROOT)
    hidden_width = expand.shape[1]
    step = min(256, hidden_width)
    reduced = None
    for start in range(0, hidden_width, step):
        hidden = gelu_scaled(dot(normed, expand[:, start : start + step])).astype(BF16)
        part = dot(hidden, reduce_weight[start : start + step, :])
        reduced = part if reduced is None else reduced + part
    return gated(attended, reduced, HALF_ROOT)


def mbconv(main, above, below, sides, conv_expand, conv_kernel, conv_reduce):
    rows, breadth, channels = main.shape
    inner = (rows + 2) * breadth
    side_rows = sides.shape[0] // 2
    x = jnp.concatenate([above, main, below], axis=0).reshape(inner, channels)
    normed = layer_norm(jnp.concatenate([x, sides], axis=0), HALF_ROOT)
    width = conv_expand.shape[1]
    step = min(256, width)
    taps = conv_kernel[...] * jnp.asarray(0.5, BF16)
    projected = None
    for start in range(0, width, step):
        e = gelu_scaled(dot(normed, conv_expand[:, start : start + step])).astype(BF16)
        body = e[:inner].reshape(rows + 2, breadth, step)
        side = e[inner:].astype(F32)
        sums, edges = [], []
        for j in range(3):
            k = [taps[3 * i + j : 3 * i + j + 1, start : start + step] for i in range(3)]
            total = body[0:rows] * k[0] + body[1 : rows + 1] * k[1] + body[2 : rows + 2] * k[2]
            sums.append(total.astype(F32))
            if j != 1:
                part = side[:side_rows] if j == 0 else side[side_rows:]
                edge = sum(part[i : i + rows] * k[i].astype(F32) for i in range(3))
                edges.append(edge.reshape(rows, 1, step))
        left = jnp.concatenate([edges[0], sums[0][:, : breadth - 1]], axis=1)
        right = jnp.concatenate([sums[2][:, 1:], edges[1]], axis=1)
        spatial = gelu_scaled(sums[1] + left + right)
        spatial = spatial.reshape(rows * breadth, step).astype(BF16)
        part = dot(spatial, conv_reduce[start : start + step, :])
        projected = part if projected is None else projected + part
    return main + projected.reshape(rows, breadth, channels) * HALF_ROOT


def band_kernel(
    first_block,
    direct,
    flags_ref,
    main_ref,
    above_ref,
    below_ref,
    top_ref,
    bottom_ref,
    sides_ref,
    grid_flags_ref,
    conv_expand,
    conv_kernel,
    conv_reduce,
    attend,
    merge,
    expand,
    reduce_weight,
    out_ref,
):
    rows, breadth, channels = main_ref.shape
    bands, per_row = rows // WIN, breadth // WIN
    step = pl.program_id(0)
    first_band = (first_block + step * CHUNKS) * bands
    last_band = flags_ref.shape[0] - bands
    above = jnp.where(first_band == 0, top_ref[...].astype(F32), above_ref[...].astype(F32))
    below = jnp.where(
        first_band == last_band, bottom_ref[...].astype(F32), below_ref[...].astype(F32)
    )
    after = mbconv(
        main_ref[...].astype(F32),
        above,
        below,
        sides_ref[0].astype(F32),
        conv_expand,
        conv_kernel,
        conv_reduce,
    )
    windows = [(t, v) for t in range(bands) for v in range(per_row)]
    x = jnp.concatenate(
        [
            after[t * WIN : (t + 1) * WIN, v * WIN : (v + 1) * WIN].reshape(PER, channels)
            for t, v in windows
        ],
        axis=0,
    )
    flags = [flags_ref[first_band + t, v].astype(F32) for t, v in windows]
    out = section(x, flags, attend, merge, expand, reduce_weight)
    square = {
        tv: out[n * PER : (n + 1) * PER].reshape(WIN, WIN, channels)
        for n, tv in enumerate(windows)
    }
    if direct:
        cols = out_ref.shape[1]
        span = breadth // cols
        for t in range(bands):
            place = step * bands + t
            start = pl.multiple_of(place * span, span)
            for group in range(cols):
                pieces = [square[t, v] for v in range(group, per_row, cols)]
                column = lax.rem(group + 2 * cols - turn(step, t), cols)
                out_ref[:, column, pl.ds(start, span)] = jnp.concatenate(pieces, axis=1).astype(
                    BF16
                )
        used = pl.num_programs(0) * bands * span
        if out_ref.shape[2] > used:
            out_ref[:, :, used:] = jnp.broadcast_to(
                grid_flags_ref[...], out_ref.shape[:2] + grid_flags_ref.shape
            )
    else:
        for t in range(bands):
            pieces = [square[t, v] for v in range(per_row)]
            out_ref[t * WIN : (t + 1) * WIN] = jnp.concatenate(pieces, axis=1).astype(BF16)


def turn(step, t):
    return step + 2 * t


def grid_static_kernel(first_block, flags_ref, x_ref, attend, merge, expand, reduce_weight, out_ref):
    bands = x_ref.shape[0]
    tokens = WIN * PER
    first_band = (first_block + pl.program_id(0) * CHUNKS) * bands
    flags = [flags_ref[first_band + t, w].astype(F32) for t in range(bands) for w in range(WIN)]
    x = jnp.concatenate([x_ref[t].astype(F32) for t in range(bands)], axis=0)
    out = section(x, flags, attend, merge, expand, reduce_weight)
    for t in range(bands):
        out_ref[t] = out[t * tokens : (t + 1) * tokens].astype(BF16)


def grid_live_kernel(
    mine_ref, x_ref, attend, merge, expand, reduce_weight, out_ref, in_ref, done_ref
):
    s = pl.program_id(0)
    shape = x_ref.shape
    tokens = WIN * PER

    @pl.when(s < mine_ref[PLACES])
    def _():
        x = x_ref[...].astype(F32).reshape(tokens, shape[-1])
        halves = range(shape[-1] // LANES)
        for n in halves:
            in_ref[n] = x[:, n * LANES : (n + 1) * LANES]
        base = WIN + mine_ref[s] * WIN

        def part(n, _):
            windows = [n * PART + w for w in range(PART)]
            spots = [pl.ds(w, PER, stride=WIN) for w in windows]
            x = jnp.concatenate(
                [jnp.concatenate([in_ref[n, spot] for n in halves], axis=1) for spot in spots],
                axis=0,
            )
            flags = [mine_ref[base + w].astype(F32) for w in windows]
            out = section(x, flags, attend, merge, expand, reduce_weight)
            for w, spot in enumerate(spots):
                for n in halves:
                    done_ref[n, spot] = out[
                        w * PER : (w + 1) * PER, n * LANES : (n + 1) * LANES
                    ]
            return 0

        lax.fori_loop(0, WIN // PART, part, 0)
        out = jnp.concatenate([done_ref[n] for n in halves], axis=1)
        out_ref[...] = out.astype(BF16).reshape(shape)


def plan_kernel(
    me_ref, flags_ref, live_ref, slots0_ref, slots1_ref, lists_ref, mine0_ref, mine1_ref, size_ref
):
    devices = flags_ref.shape[0]
    cols = devices // WIN
    me = me_ref[0]

    def source(h, place, c):
        step, t = divmod(place, STEP_BANDS)
        band = (h + step * CHUNKS) * STEP_BANDS + t
        return band * cols + lax.rem(c + turn(step, t), cols)

    most = []
    for h, slots_ref, mine_ref in ((0, slots0_ref, mine0_ref), (1, slots1_ref, mine1_ref)):

        def one(d, top, h=h, slots_ref=slots_ref):
            i, c = d // cols, lax.rem(d, cols)
            count = jnp.int32(0)
            for place in range(PLACES):
                live = live_ref[source(h, place, c), i] != 0
                slots_ref[place * devices + d] = jnp.where(live, count, -1)
                if h == 1:
                    lists_ref[d * PLACES + place] = 0
                    lists_ref[d * PLACES + count] = jnp.where(live, place, 0)
                count = count + jnp.where(live, 1, 0)
            return jnp.maximum(top, count)

        most.append(lax.fori_loop(0, devices, one, jnp.int32(0)))
        row, column = me // cols, lax.rem(me, cols)
        count = jnp.int32(0)
        for place in range(PLACES):
            at = source(h, place, column)
            live = live_ref[at, row] != 0
            mine_ref[place] = 0
            mine_ref[count] = jnp.where(live, place, 0)
            count = count + jnp.where(live, 1, 0)
            for w in range(WIN):
                mine_ref[WIN + place * WIN + w] = flags_ref[at, row * WIN + w]
        mine_ref[PLACES] = count
    size = jnp.int32(len(SIZES) - 1)
    for n in reversed(range(len(SIZES) - 1)):
        fits = (most[0] <= SIZES[n][0]) & (most[1] <= SIZES[n][1])
        size = jnp.where(fits, n, size)
    size_ref[0] = size


def pack_kernel(lists_ref, x_ref, out_ref):
    span = x_ref.shape[1] // PLACES
    slots = out_ref.shape[1] // span
    base = pl.program_id(0) * x_ref.shape[0]

    def one(d, _):
        for s in range(slots):
            place = lists_ref[(base + d) * PLACES + s]
            start = pl.multiple_of(place * span, span)
            out_ref[d, s * span : (s + 1) * span] = x_ref[d, pl.ds(start, span)]
        return 0

    lax.fori_loop(0, x_ref.shape[0], one, 0, unroll=4)


def merge_kernel(slots_ref, back_ref, own_ref, _, out_ref):
    devices = back_ref.shape[0]
    cols = devices // WIN
    span = out_ref.shape[2] // cols
    step = pl.program_id(0)
    for t in range(STEP_BANDS):
        place = step * STEP_BANDS + t
        mine = pl.multiple_of(place * span, span)

        def one(i, _, t=t, place=place, mine=mine):
            blocks = []
            for group in range(cols):
                device = i * cols + lax.rem(group + 2 * cols - turn(step, t), cols)
                slot = slots_ref[place * devices + device]
                start = pl.multiple_of(jnp.maximum(slot, 0) * span, span)
                there = back_ref[device, pl.ds(start, span)].astype(F32)
                here = own_ref[device, pl.ds(mine, span)].astype(F32)
                blocks.append(jnp.where(slot >= 0, there, here))
            pieces = [
                b[h * WIN : (h + 1) * WIN] for h in range(span // WIN) for b in blocks
            ]
            out_ref[0, t * WIN + i] = jnp.concatenate(pieces, axis=0).astype(BF16)
            return 0

        lax.fori_loop(0, WIN, one, 0, unroll=2)


def whole(array):
    return pl.BlockSpec(array.shape, lambda *_: (0,) * array.ndim)


def shift(array, axis, up):
    size = lax.axis_size(axis)
    pairs = [(i, i + 1) for i in range(size - 1)]
    return lax.ppermute(array, axis, pairs if up else [(j, i) for i, j in pairs])


PARAMS = pltpu.CompilerParams(vmem_limit_bytes=60 << 20)


def along(shape, axis, size):
    block = shape[:axis] + (size,) + shape[axis + 1 :]
    return pl.BlockSpec(
        block, lambda i, f: (0,) * axis + (i,) + (0,) * (len(shape) - axis - 1)
    )


def call(kernel, steps, flags, specs, arrays, shape, out_spec, name, aliases={}, scratch=()):
    return pl.pallas_call(
        kernel,
        out_shape=jax.ShapeDtypeStruct(shape, BF16),
        grid_spec=pltpu.PrefetchScalarGridSpec(
            num_scalar_prefetch=1, grid=(steps,), in_specs=specs, out_specs=out_spec,
            scratch_shapes=scratch,
        ),
        compiler_params=PARAMS,
        input_output_aliases=aliases,
        name=name,
    )(flags, *arrays)


def feature_halo(features):
    height, breadth, _ = features.shape
    top = shift(features[height - 1 :], "row", True)
    bottom = shift(features[:1], "row", False)
    edge_columns = [
        jnp.concatenate([top[:, c], features[:, c], bottom[:, c]], axis=0) for c in (0, breadth - 1)
    ]
    left = shift(edge_columns[1], "col", True)
    right = shift(edge_columns[0], "col", False)
    return top, bottom, left, right


def exchange(array):
    return lax.all_to_all(array, ("row", "col"), split_axis=0, concat_axis=0, tiled=True)


def on_device(
    features,
    conv_expand,
    conv_kernel,
    conv_reduce,
    block_attend,
    block_merge,
    block_expand,
    block_reduce,
    grid_attend,
    grid_merge,
    grid_expand,
    grid_reduce,
    block_valid,
    grid_valid,
):
    height, breadth, channels = features.shape
    rows, cols = lax.axis_size("row"), lax.axis_size("col")
    devices = rows * cols
    parity = rows // GRID
    direct = parity == 1 and breadth % (2 * WIN * cols) == 0
    step_rows = STEP_BANDS * WIN
    steps = height // step_rows // CHUNKS
    per_chunk = steps * STEP_BANDS
    direct = direct and per_chunk == PLACES
    conv_weights = (conv_expand, conv_kernel, conv_reduce)
    block_weights = (block_attend, block_merge, block_expand, block_reduce)
    grid_weights = (grid_attend, grid_merge, grid_expand, grid_reduce)

    top, bottom, left, right = feature_halo(features)
    padded = -(-(step_rows + 2) // 8) * 8
    gap = jnp.zeros((padded - step_rows - 2, channels), BF16)
    sides = jnp.stack(
        [
            jnp.concatenate([left[r : r + step_rows + 2], gap, right[r : r + step_rows + 2], gap])
            for r in range(0, height, step_rows)
        ]
    )
    flag_row = jnp.pad(
        grid_valid.reshape(WIN, WIN).astype(BF16), ((0, 0), (0, channels - WIN))
    )
    row_block = (1, breadth, channels)

    def blocks_of(h):
        arrays = [features, features, features, top, bottom, sides, flag_row]
        arrays += [*conv_weights, *block_weights]

        def row_at(offset):
            def index(i, f):
                row = (h + i * CHUNKS) * step_rows + offset
                return jnp.clip(row, 0, height - 1), 0, 0

            return pl.BlockSpec(row_block, index)

        specs = [
            pl.BlockSpec((step_rows, breadth, channels), lambda i, f: (h + i * CHUNKS, 0, 0)),
            row_at(-1),
            row_at(step_rows),
            whole(top),
            whole(bottom),
            pl.BlockSpec((1, *sides.shape[1:]), lambda i, f: (h + i * CHUNKS, 0, 0)),
        ] + [whole(a) for a in arrays[6:]]
        if direct:
            extra = flag_row.shape[0] if h == 0 else 0
            shape = (rows, cols, per_chunk * (breadth // cols) + extra, channels)
            out_spec = pl.BlockSpec(shape, lambda i, f: (0, 0, 0, 0))
        else:
            shape = (steps * step_rows, breadth, channels)
            out_spec = along(shape, 0, step_rows)
        kernel = functools.partial(band_kernel, h, direct)
        return call(kernel, steps, block_valid, specs, arrays, shape, out_spec, "conv_and_blocks")

    if direct:
        return live_groups(blocks_of, grid_weights, (height, breadth, channels), rows, cols)

    repeat = breadth // (WIN * cols)
    part = WIN // parity
    me = lax.axis_index("row")
    flags = grid_valid[:, :, 0, :]
    spread = exchange(jnp.broadcast_to(flags[None], (devices, *flags.shape)))
    spread = spread.reshape(rows, cols, *flags.shape)
    spread = lax.dynamic_index_in_dim(spread, lax.axis_index("col"), 1, keepdims=False)
    by_band = jnp.transpose(spread, (1, 0, 2, 3)).reshape(parity, height // WIN, WIN, WIN)
    mine = lax.dynamic_index_in_dim(by_band, me // parity, 2, keepdims=False)
    mine = lax.dynamic_slice_in_dim(mine, (me % parity) * part, part, 2)
    grid_flags = jnp.transpose(mine, (1, 0, 2)).reshape(height // WIN, WIN)
    outputs = []
    for h in range(CHUNKS):
        split = blocks_of(h).reshape(per_chunk, WIN, repeat, cols, parity, part, channels)
        sending = jnp.transpose(split, (1, 4, 3, 0, 2, 5, 6))
        arrived = exchange(sending.reshape(devices, per_chunk, repeat * part, channels))
        split = arrived.reshape(GRID, parity, cols, per_chunk, repeat, part, channels)
        arrived = jnp.transpose(split, (3, 1, 5, 0, 2, 4, 6))
        arrived = arrived.reshape(per_chunk, WIN * PER, channels)
        spec = along(arrived.shape, 0, STEP_BANDS)
        finished = call(
            functools.partial(grid_static_kernel, h),
            steps,
            grid_flags,
            [spec] + [whole(a) for a in grid_weights],
            [arrived, *grid_weights],
            arrived.shape,
            spec,
            "grid_section",
        )
        split = finished.reshape(per_chunk, parity, part, GRID, cols, repeat, channels)
        finished = jnp.transpose(split, (3, 1, 4, 0, 5, 2, 6))
        returned = exchange(finished.reshape(devices, per_chunk, repeat * part, channels))
        split = returned.reshape(WIN, parity, cols, per_chunk, repeat, part, channels)
        spread = jnp.transpose(split, (3, 0, 4, 2, 1, 5, 6))
        outputs.append(spread.reshape(steps, step_rows, breadth, channels))
    return jnp.stack(outputs, axis=1).reshape(height, breadth, channels)


def live_groups(blocks_of, grid_weights, tile, rows, cols):
    height, breadth, channels = tile
    devices = rows * cols
    span = breadth // cols
    step_rows = STEP_BANDS * WIN
    steps = PLACES // STEP_BANDS
    smem = pl.BlockSpec(memory_space=pltpu.SMEM)
    first = blocks_of(0).reshape(devices, -1, channels)
    arrived = exchange(first)
    second = blocks_of(1).reshape(devices, -1, channels)
    square = arrived[:, PLACES * span : PLACES * span + WIN, :WIN].astype(jnp.int32)
    live = jnp.max(square, axis=2)
    flags = square.reshape(devices, WIN * WIN)
    me = (lax.axis_index("row") * cols + lax.axis_index("col")).reshape(1)
    table = jax.ShapeDtypeStruct((PLACES * devices,), jnp.int32)
    own = jax.ShapeDtypeStruct((WIN + PLACES * WIN,), jnp.int32)
    *plan, size = pl.pallas_call(
        plan_kernel,
        out_shape=(table, table, table, own, own, jax.ShapeDtypeStruct((1,), jnp.int32)),
        in_specs=[smem] * 3,
        out_specs=(smem,) * 6,
        name="plan",
    )(me, flags, live)

    def branch(counts):
        block = (devices, span, channels)
        by_slot = pl.BlockSpec(block, lambda s, m: (0, s, 0))
        by_place = pl.BlockSpec(block, lambda s, m: (0, m[s], 0))
        shapes = [(devices, count * span, channels) for count in counts]

        def sections(h, x, spec, mine, weights):
            arrays = [x, *weights]
            specs = [spec] + [whole(a) for a in weights]
            return call(
                grid_live_kernel, counts[h], mine, specs, arrays, shapes[h], by_slot,
                "grid_section",
                scratch=(
                    pltpu.VMEM((channels // LANES, WIN * PER, LANES), F32),
                    pltpu.VMEM((channels // LANES, WIN * PER, LANES), F32),
                ),
            )

        def merged(h, slots, back, own, base):
            out_shape = (CHUNKS * steps, step_rows, breadth, channels)
            out_spec = pl.BlockSpec(
                (1, *out_shape[1:]), lambda i, f: (h + i * CHUNKS, 0, 0, 0)
            )
            specs = [whole(back), whole(own), pl.BlockSpec(memory_space=pl.ANY)]
            return call(
                merge_kernel, steps, slots, specs, [back, own, base], out_shape, out_spec,
                "merge", {} if h == 0 else {3: 0},
            )

        def run(first, arrived, second, slots0, slots1, lists, mine0, mine1, *weights):
            packed = call(
                pack_kernel, 4, lists, [along((devices // 4, *second.shape[1:]), 0, devices // 4)],
                [second], shapes[1], along((devices // 4, *shapes[1][1:]), 0, devices // 4), "pack",
            )
            other = exchange(packed)
            back = exchange(sections(0, arrived, by_place, mine0, weights))
            other = exchange(sections(1, other, by_slot, mine1, weights))
            out = merged(0, slots0, back, first, back)
            return merged(1, slots1, other, second, out)

        return run

    out = lax.switch(
        size[0], [branch(counts) for counts in SIZES], first, arrived, second, *plan, *grid_weights
    )
    return out.reshape(height, breadth, channels)


def solution(mesh):
    in_specs = (P("row", "col", None),) + (P(),) * 11
    in_specs += (P("row", "col"), P(None, "row", None, "col"))
    return jax.shard_map(
        on_device,
        mesh=mesh,
        in_specs=in_specs,
        out_specs=P("row", "col", None),
        check_vma=False,
    )
```
